256 devices in a mesh: phi: 64 (over z, x, y_lo), row: 4 (over y_hi, core).
Axes of the slice: x: 4, y: 4 (y_hi: 2, y_lo: 2; y = y_hi * 2 + y_lo), z: 8, core: 2. Of those that a mesh axis runs over, the one named last changes fastest.
Arguments:
- density: float32 [1024, 32, 512], P('phi', None, 'row'), may hold values from 0.5 to 2
- velocity: float32 [3, 1024, 32, 512], P(None, 'phi', None, 'row'), may hold values from -0.3 to 0.3
- shifts: int32 [64], P('row'), may hold values from 0 to 255, as said below
- fractions: float32 [64], P('row'), may hold values from 0 to 1
Outputs:
- density_out: float32 [1024, 32, 512], P('phi', None, 'row')
- stepped_velocity: float32 [3, 1024, 32, 512], P(None, 'phi', None, 'row')
- image: float32 [1024, 1024], P(('phi', 'row'))
The draws below stay inside these ranges and needn't reach their ends.
Inputs may be any that keep to these rules, and one draw needn't show every extreme that they name: `shifts`: some band has shift 0 and some band has shift 256 - 1.
All inputs are finite; a program needn't handle non-finite values.
Results may differ from the reference program's by a relative error of at most 0.000071.
Values sent between devices are 32-bit elements; how exact they have to be, the bound alone decides.
A program may use at most 64 MiB of HBM per device.

```python
import jax
import jax.numpy as jnp
from jax import lax

NTH = 32
BAND = 8
STEPS = 2
NPIX = 1024
NPHI = 1024
NR = 512
NBANDS = 64
SHIFT_MAX = 256


def draw_shifts(key, part):
    first, second, third = jax.random.split(jax.random.fold_in(key, 17), 3)
    values = jax.random.randint(first, (NBANDS,), 0, SHIFT_MAX)
    top = jax.random.randint(second, (), 0, NBANDS)
    low = (top + 1 + jax.random.randint(third, (), 0, NBANDS - 1)) % NBANDS
    values = values.at[top].set(SHIFT_MAX - 1)
    values = values.at[low].set(0)
    return values.astype(jnp.int32)


def shard_levels(stream_key, extent, shards, low, high):
    loudness = 1.0
    for position, shards_of in shards:
        steps = jax.random.uniform(jax.random.fold_in(jax.random.fold_in(stream_key, 6), position), (shards_of,), jnp.float32, low / len(shards), high / len(shards))
        loudness = loudness * jnp.repeat(jnp.exp(steps), extent[position] // shards_of).reshape((-1,) + (1,) * (len(extent) - 1 - position))
    return loudness


def setup_inputs(seed: int = 0) -> dict:
    splits = jax.random.split(jax.random.key(seed), 5)
    return {
        "density": jnp.clip(0.5 + 1.5 * jax.random.uniform(splits[0], (NPHI, NTH, NR), jnp.float32) ** shard_levels(splits[0], (NPHI, NTH, NR), ((0, 64), (2, 4)), -0.2, 0.2), 0.5, 2.0),
        "velocity": jnp.clip(jax.random.uniform(splits[1], (3, NPHI, NTH, NR), jnp.float32, -0.3, 0.3) * shard_levels(splits[1], (3, NPHI, NTH, NR), ((1, 64), (3, 4)), -0.4, 0.0), -0.3, 0.3),
        "shifts": draw_shifts(jax.random.fold_in(splits[4], 71), 0),
        "fractions": jnp.clip(1.0 * jax.random.uniform(splits[3], (NBANDS,), jnp.float32) ** shard_levels(splits[3], (NBANDS,), ((0, 4),), -0.2, 0.2), 0.0, 1.0),
    }


SPEED = 1.5
COURANT = 0.05
KAPPA = 1.5
R_INNER = 0.2

def conserved(prim):
    rho = prim[0]
    return jnp.stack([rho, rho * prim[1], rho * prim[2], rho * prim[3]])

def divergence(extended, axis, comp):
    cons = conserved(extended)
    flux = cons * extended[comp][None]
    flux = flux.at[comp].add(extended[0])
    size = extended.shape[axis]
    low_c = lax.slice_in_dim(cons, 0, size - 1, axis=axis)
    high_c = lax.slice_in_dim(cons, 1, size, axis=axis)
    low_f = lax.slice_in_dim(flux, 0, size - 1, axis=axis)
    high_f = lax.slice_in_dim(flux, 1, size, axis=axis)
    face = 0.5 * (low_f + high_f) - 0.5 * SPEED * (high_c - low_c)
    return lax.slice_in_dim(face, 1, size - 1, axis=axis) - lax.slice_in_dim(face, 0, size - 2, axis=axis)

def advance(prim, ext_phi, padded_polar_grid, ext_radial):
    total = divergence(ext_phi, 1, 2) + divergence(padded_polar_grid, 2, 3) + divergence(ext_radial, 3, 1)
    fresh = conserved(prim) - COURANT * total
    rho = fresh[0]
    return jnp.stack([rho, fresh[1] / rho, fresh[2] / rho, fresh[3] / rho])

def column_light(rho, radial_index, total_radial):
    polar = rho.shape[1]
    dtau = KAPPA / polar * rho
    above = jnp.cumsum(dtau, axis=1) - dtau
    theta = (jnp.arange(polar, dtype=jnp.int32).astype(jnp.float32) + 0.5) / polar
    tilt = 1.0 + 0.5 * jnp.cos(jnp.pi * theta)
    radius = R_INNER + (radial_index.astype(jnp.float32) + 0.5) * (1.0 - R_INNER) / total_radial
    source = (1.0 / jnp.sqrt(radius))[None, None, :] * tilt[None, :, None]
    return lax.optimization_barrier(jnp.sum(source * (1.0 - jnp.exp(-dtau)) * jnp.exp(-above), axis=1))

def pixel_corners(pixel_rows, npix, nphi, nrad):
    yy = ((pixel_rows.astype(jnp.float32) + 0.5) / npix * 2.0 - 1.0)[:, None]
    xx = ((jnp.arange(npix, dtype=jnp.int32).astype(jnp.float32) + 0.5) / npix * 2.0 - 1.0)[None, :]
    dist = jnp.sqrt(xx * xx + yy * yy)
    upos = (dist - R_INNER) / (1.0 - R_INNER) * nrad - 0.5
    radial_floor_index = jnp.floor(upos)
    radial_fraction = upos - radial_floor_index
    radial_lower_index = radial_floor_index.astype(jnp.int32)
    angle = jnp.arctan2(yy, xx)
    vpos = (angle + jnp.pi) / (2.0 * jnp.pi) * nphi - 0.5
    lfloor = jnp.floor(vpos)
    polar_fraction = vpos - lfloor
    polar_lower_index = lfloor.astype(jnp.int32) % nphi
    polar_upper_index = (polar_lower_index + 1) % nphi
    return [(polar_lower_index, radial_lower_index, (1.0 - polar_fraction) * (1.0 - radial_fraction)), (polar_upper_index, radial_lower_index, polar_fraction * (1.0 - radial_fraction)), (polar_lower_index, radial_lower_index + 1, (1.0 - polar_fraction) * radial_fraction), (polar_upper_index, radial_lower_index + 1, polar_fraction * radial_fraction)]

def sample_block(table, corners, l_first, k_first):
    nl, nk = table.shape
    flat = table.reshape(-1)
    total = jnp.zeros(corners[0][2].shape, table.dtype)
    for lidx, kidx, weight in corners:
        lloc = lidx - l_first
        kloc = kidx - k_first
        valid = (lloc >= 0) & (lloc < nl) & (kloc >= 0) & (kloc < nk)
        spot = jnp.clip(lloc, 0, nl - 1) * nk + jnp.clip(kloc, 0, nk - 1)
        total = total + jnp.where(valid, weight * jnp.take(flat, spot), 0.0)
    return total

def reference(density, velocity, shifts, fractions):
    prim = jnp.concatenate([density[None], velocity], axis=0)
    nphi = prim.shape[1]
    nrad = prim.shape[3]
    shift_col = jnp.repeat(shifts, BAND)
    frac_col = jnp.repeat(fractions, BAND)
    cells = jnp.arange(nphi, dtype=jnp.int32)[:, None]
    src_a = (cells - shift_col[None, :]) % nphi
    src_b = (cells - shift_col[None, :] - 1) % nphi
    idx_a = jnp.broadcast_to(src_a[None, :, None, :], prim.shape)
    idx_b = jnp.broadcast_to(src_b[None, :, None, :], prim.shape)
    for step in range(STEPS):
        ext_phi = jnp.pad(prim, ((0, 0), (1, 1), (0, 0), (0, 0)), mode='wrap')
        padded_polar_grid = jnp.pad(prim, ((0, 0), (0, 0), (1, 1), (0, 0)))
        ext_radial = jnp.pad(prim, ((0, 0), (0, 0), (0, 0), (1, 1)))
        prim = advance(prim, ext_phi, padded_polar_grid, ext_radial)
        prim = (1.0 - frac_col) * jnp.take_along_axis(prim, idx_a, axis=1) + frac_col * jnp.take_along_axis(prim, idx_b, axis=1)
    intensity = column_light(prim[0], jnp.arange(nrad, dtype=jnp.int32), nrad)
    corners = pixel_corners(jnp.arange(NPIX, dtype=jnp.int32), NPIX, nphi, nrad)
    image = sample_block(intensity, corners, 0, 0)
    return (prim[0], prim[1:], image)
```

```python
import functools

import jax
import jax.numpy as jnp
import numpy as np
from jax import lax
from jax.experimental import pallas as pl
from jax.experimental.pallas import tpu as pltpu
from jax.sharding import PartitionSpec as P

MESH = pl.DeviceIdType.MESH
BAND = 8
NPIX = 1024
NPHI = 1024
NR = 512
NTH = 32
KAPPA = 1.5
R_INNER = 0.2
F32 = jnp.float32
VM = pl.BlockSpec(memory_space=pltpu.VMEM)
SM = pl.BlockSpec(memory_space=pltpu.SMEM)
ANY = pl.BlockSpec(memory_space=pl.ANY)


def where_of(band, group):
    return (band % 8) * 8 + group * 2 + band // 8


def lanes():
    return lax.broadcasted_iota(jnp.int32, (8, 128), 1)


def conserved(q):
    return [q[0], q[0] * q[1], q[0] * q[2], q[0] * q[3]]


def side(q, comp, offset):
    m = q[0] * (0.5 * q[comp] + offset)
    out = [m, m * q[1], m * q[2], m * q[3]]
    out[comp] = out[comp] + 0.5 * q[0]
    return out


def updated(here, lower, upper):
    total = None
    for (comp, low), (_, high) in zip(lower, upper):
        p, m = side(low, comp, 0.75), side(high, comp, -0.75)
        part = [b - a for a, b in zip(p, m)]
        total = part if total is None else [s + t for s, t in zip(total, part)]
    new = [0.775 * c - 0.05 * t for c, t in zip(conserved(here), total)]
    inv = 1.0 / new[0]
    return [new[0], new[1] * inv, new[2] * inv, new[3] * inv]


def to_tiles_kernel(rho_ref, vel_ref, out_ref, edge_ref):
    for f in range(4):
        for g in range(4):
            src = rho_ref[:, 8 * g : 8 * g + 8, :] if f == 0 else vel_ref[f - 1, :, 8 * g : 8 * g + 8, :]
            t = src.reshape(128, 128).T
            out_ref[f, g] = t
            edge_ref[0, pl.ds(f * 4 + g, 1), :] = t[0:1, :]
            edge_ref[1, pl.ds(f * 4 + g, 1), :] = t[127:128, :]


def greet(peers):
    bar = pltpu.get_barrier_semaphore()
    for peer in peers:
        pl.semaphore_signal(bar, inc=1, device_id=peer, device_id_type=MESH)
    pl.semaphore_wait(bar, len(peers))


def first_edges_kernel(rho_ref, vel_ref, edge_ref, hphi_ref, hr_ref, ssem, rsem):
    phi, row = lax.axis_index("phi"), lax.axis_index("row")
    left, right = {"phi": lax.rem(phi + 63, 64)}, {"phi": lax.rem(phi + 1, 64)}
    below, above = {"row": lax.rem(row + 3, 4)}, {"row": lax.rem(row + 1, 4)}
    greet((left, right, below, above))

    def copy(i, src, dst, to):
        return pltpu.make_async_remote_copy(src, dst, ssem.at[i], rsem.at[i], device_id=to, device_id_type=MESH)

    copies = [
        copy(0, rho_ref.at[15], hphi_ref.at[0, 0], right),
        copy(1, vel_ref.at[:, 15], hphi_ref.at[0, pl.ds(1, 3)], right),
        copy(2, rho_ref.at[0], hphi_ref.at[1, 0], left),
        copy(3, vel_ref.at[:, 0], hphi_ref.at[1, pl.ds(1, 3)], left),
        copy(4, edge_ref.at[1], hr_ref.at[0], above),
        copy(5, edge_ref.at[0], hr_ref.at[1], below),
    ]
    for c in copies:
        c.start()
    for c in copies:
        c.wait()


def first_hydro_kernel(ends_ref, a_ref, hphi_ref, hr_ref, out_ref, pad, ht):
    has_low = (ends_ref[0] > 0).astype(F32)
    has_high = (ends_ref[1] > 0).astype(F32)
    for pair in range(2):
        x = jnp.concatenate(
            [hphi_ref[s, 2 * pair + f] for f in range(2) for s in range(2)], axis=0
        )
        ht[pair] = x.T
    for f in range(4):
        for g in range(4):
            pad[f, g, 8:136, :] = a_ref[f, g]
            pad[f, g, 7:8, :] = hr_ref[0, pl.ds(f * 4 + g, 1), :] * has_low
            pad[f, g, 136:137, :] = hr_ref[1, pl.ds(f * 4 + g, 1), :] * has_high
    lane = lanes()
    first, last = lane < 8, lane >= 120
    low_th, high_th = (lane % 8) == 0, (lane % 8) == 7

    def step(j, carry):
        base = pl.multiple_of(8 * j, 8)
        here = [[pad[f, g, pl.ds(base + 8, 8), :] for f in range(4)] for g in range(4)]
        edge = [ht[pair, pl.ds(base, 8), :] for pair in range(2)]
        for g in range(4):
            c = here[g]
            before = [pad[f, g, pl.ds(base, 16), :][7:15] for f in range(4)]
            after = [pad[f, g, pl.ds(base + 8, 16), :][1:9] for f in range(4)]
            thm, thp, phm, php = [], [], [], []
            for f in range(4):
                lo = pltpu.roll(here[g - 1][f], 121, 1) if g > 0 else jnp.zeros((8, 128), F32)
                hi = pltpu.roll(here[g + 1][f], 7, 1) if g < 3 else jnp.zeros((8, 128), F32)
                thm.append(jnp.where(low_th, lo, pltpu.roll(c[f], 1, 1)))
                thp.append(jnp.where(high_th, hi, pltpu.roll(c[f], 127, 1)))
                off = (f % 2) * 64 + g * 8
                lo = pltpu.roll(edge[f // 2], (128 - off) % 128, 1)
                hi = pltpu.roll(edge[f // 2], (120 - off - 32) % 128, 1)
                phm.append(jnp.where(first, lo, pltpu.roll(c[f], 8, 1)))
                php.append(jnp.where(last, hi, pltpu.roll(c[f], 120, 1)))
            new = updated(c, ((2, phm), (3, thm), (1, before)), ((2, php), (3, thp), (1, after)))
            d = lax.rem(j, 8) * 8 + g * 2 + j // 8
            for f in range(4):
                out_ref[d, f] = new[f]
        return carry

    lax.fori_loop(0, 16, step, 0)


def a2a_kernel(x_ref, o_ref, send_sem, recv_sem, loc_sem):
    me = lax.axis_index("phi")
    bar = pltpu.get_barrier_semaphore()

    def sig(d, c):
        pl.semaphore_signal(bar, inc=1, device_id={"phi": lax.rem(me + d, 64)}, device_id_type=MESH)
        return c

    lax.fori_loop(1, 64, sig, 0)
    pl.semaphore_wait(bar, 63)

    def copy(d):
        t = lax.rem(me + d, 64)
        return pltpu.make_async_remote_copy(
            x_ref.at[t], o_ref.at[me], send_sem.at[d], recv_sem.at[d],
            device_id={"phi": t}, device_id_type=MESH,
        )

    own = pltpu.make_async_copy(x_ref.at[me], o_ref.at[me], loc_sem)
    own.start()

    def go(i, c):
        copy(i).start()
        copy(64 - i).start()
        return c

    lax.fori_loop(1, 32, go, 0)
    copy(32).start()

    def done(d, c):
        copy(d).wait()
        return c

    lax.fori_loop(1, 64, done, 0)
    own.wait()


def all_to_all(x, cid):
    return pl.pallas_call(
        a2a_kernel,
        name="a2a",
        out_shape=jax.ShapeDtypeStruct(x.shape, x.dtype),
        in_specs=[ANY],
        out_specs=ANY,
        scratch_shapes=[pltpu.SemaphoreType.DMA((64,)), pltpu.SemaphoreType.DMA((64,)), pltpu.SemaphoreType.DMA],
        compiler_params=pltpu.CompilerParams(collective_id=cid, has_side_effects=True),
    )(x)


def advect(src, dst, ints, frac):
    whole, remain = ints[0], ints[1]
    w = frac[0]
    lane = lanes()
    one, two = 8 * remain, 8 * (remain + 1)
    two_roll = lax.rem(two, 128)
    keep_one, keep_two = lane >= one, lane >= two

    def rolled(p):
        slab = lax.rem(p + 128 - whole, 64)
        tiles = [src[slab, f] for f in range(4)]
        return [pltpu.roll(t, one, 1) for t in tiles] + [pltpu.roll(t, two_roll, 1) for t in tiles]

    def step(p, prev):
        cur = rolled(p)
        for f in range(4):
            lead = jnp.where(keep_one, cur[f], prev[f])
            trail = jnp.where(keep_two, cur[4 + f], prev[4 + f])
            dst[p, f] = (1.0 - w) * lead + w * trail
        return cur

    lax.fori_loop(0, 64, step, rolled(-1), unroll=2)


def first_advect_kernel(ints, frac, src, out, th_ref, r_ref):
    advect(src, out, ints, frac)
    lane8 = lanes() % 8

    def step(big, carry):
        for f in range(4):
            top = bottom = None
            for j in range(8):
                t = out[big * 8 + j, f]
                hi = pltpu.roll(t, (j - 7) % 128, 1)
                lo = pltpu.roll(t, j, 1)
                top = hi if top is None else jnp.where(lane8 == j, hi, top)
                bottom = lo if bottom is None else jnp.where(lane8 == j, lo, bottom)
                r_ref[0, big * 8 + j, pl.ds(f, 1), :] = t[0:1, :]
                r_ref[1, big * 8 + j, pl.ds(f, 1), :] = t[7:8, :]
            th_ref[0, big, f] = bottom
            th_ref[1, big, f] = top
        return carry

    lax.fori_loop(0, 8, step, 0)


def second_edges_kernel(th_ref, r_ref, hth_ref, hr_ref, ssem, rsem):
    phi, row = lax.axis_index("phi"), lax.axis_index("row")
    z, x, y = phi // 8, lax.rem(phi // 2, 4), lax.rem(phi, 2)
    band = row * 16 + y * 8 + z

    def at_band(b):
        j = lax.rem(b, 16)
        return {"phi": lax.rem(j, 8) * 8 + x * 2 + j // 8, "row": b // 16}

    def at_group(g):
        return {"phi": z * 8 + g * 2 + y}

    below, above = at_band(lax.rem(band + 63, 64)), at_band(lax.rem(band + 1, 64))
    left, right = at_group(lax.rem(x + 3, 4)), at_group(lax.rem(x + 1, 4))
    greet((below, above, left, right))

    def copy(i, src, dst, to):
        return pltpu.make_async_remote_copy(src, dst, ssem.at[i], rsem.at[i], device_id=to, device_id_type=MESH)

    copies = [
        copy(0, r_ref.at[1], hr_ref.at[0], above),
        copy(1, r_ref.at[0], hr_ref.at[1], below),
        copy(2, th_ref.at[1], hth_ref.at[0], right),
        copy(3, th_ref.at[0], hth_ref.at[1], left),
    ]
    for c in copies:
        c.start()
    for c in copies:
        c.wait()


def second_hydro_kernel(ints, frac, src, hth_ref, hr_ref, out, mid):
    scale = [(ints[i] > 0).astype(F32) for i in range(2, 6)]
    lane = lanes()
    sub = lax.broadcasted_iota(jnp.int32, (8, 128), 0)
    first, last = lane < 8, lane >= 120
    low_th, high_th = (lane % 8) == 0, (lane % 8) == 7
    low_r, high_r = sub == 0, sub == 7

    def step(big, carry):
        packed = [[hth_ref[s, big, f] * scale[2 + s] for f in range(4)] for s in range(2)]
        for j in range(8):
            p = big * 8 + j
            before, after = lax.rem(p + 63, 64), lax.rem(p + 1, 64)
            c = [src[p, f] for f in range(4)]
            thm, thp, phm, php, rm, rp = [], [], [], [], [], []
            for f in range(4):
                thm.append(jnp.where(low_th, pltpu.roll(packed[0][f], (-j) % 128, 1), pltpu.roll(c[f], 1, 1)))
                thp.append(jnp.where(high_th, pltpu.roll(packed[1][f], 7 - j, 1), pltpu.roll(c[f], 127, 1)))
                phm.append(jnp.where(first, pltpu.roll(src[before, f], 8, 1), pltpu.roll(c[f], 8, 1)))
                php.append(jnp.where(last, pltpu.roll(src[after, f], 120, 1), pltpu.roll(c[f], 120, 1)))
                lo = hr_ref[0, p, pl.ds(f, 1), :] * scale[0]
                hi = hr_ref[1, p, pl.ds(f, 1), :] * scale[1]
                rm.append(jnp.where(low_r, jnp.broadcast_to(lo, (8, 128)), pltpu.roll(c[f], 1, 0)))
                rp.append(jnp.where(high_r, jnp.broadcast_to(hi, (8, 128)), pltpu.roll(c[f], 7, 0)))
            new = updated(c, ((2, phm), (3, thm), (1, rm)), ((2, php), (3, thp), (1, rp)))
            for f in range(4):
                mid[p, f] = new[f]
        return carry

    lax.fori_loop(0, 8, step, 0)
    advect(mid, out, ints, frac)


def from_tiles_kernel(row_ref, src, rho_ref, vel_ref, light_ref, flat):
    for f in range(4):
        for g in range(4):
            x = jnp.concatenate([src[where_of(j, g), f] for j in range(16)], axis=0)
            t = x.T.reshape(16, 8, 128)
            if f == 0:
                rho_ref[:, 8 * g : 8 * g + 8, :] = t
                for i in range(16):
                    flat[pl.ds(i * 32 + 8 * g, 8), :] = t[i]
            else:
                vel_ref[f - 1, :, 8 * g : 8 * g + 8, :] = t
    k = row_ref[0] * 128 + lax.broadcasted_iota(jnp.int32, (16, 128), 1)
    radius = R_INNER + (k.astype(F32) + 0.5) * (1.0 - R_INNER) / NR
    base = 1.0 / jnp.sqrt(radius)
    seen = jnp.ones((16, 128), F32)
    total = jnp.zeros((16, 128), F32)
    for j in range(NTH):
        tilt = float(np.float32(1.0 + 0.5 * np.cos(np.pi * (j + 0.5) / NTH)))
        t = jnp.exp(flat[pl.ds(j, 16, stride=32), :] * (-KAPPA / NTH))
        total = total + tilt * ((1.0 - t) * seen)
        seen = seen * t
    light_ref[...] = base * total


def gather_kernel(x_ref, w_ref, ssem, rsem, loc_sem):
    phi, row = lax.axis_index("phi"), lax.axis_index("row")
    z, xy = phi // 8, lax.rem(phi, 8)
    me = xy * 4 + row
    bar = pltpu.get_barrier_semaphore()

    def plane(d):
        m = lax.rem(me + d, 32)
        return {"phi": z * 8 + m // 4, "row": lax.rem(m, 4)}

    def column(d):
        return {"phi": lax.rem(z + d, 8) * 8 + xy}

    def sig(d, c):
        pl.semaphore_signal(bar, inc=1, device_id=plane(d), device_id_type=MESH)
        return c

    lax.fori_loop(1, 32, sig, 0)
    for d in range(1, 8):
        pl.semaphore_signal(bar, inc=1, device_id=column(d), device_id_type=MESH)
    pl.semaphore_wait(bar, 38)
    mine = w_ref.at[row, z, xy]
    own = pltpu.make_async_copy(x_ref, mine, loc_sem)
    own.start()

    def up(d):
        return pltpu.make_async_remote_copy(
            x_ref, mine, ssem.at[32 + d], rsem.at[32 + d], device_id=column(d), device_id_type=MESH
        )

    for d in range(1, 8):
        up(d).start()
    for d in range(1, 8):
        up(d).wait()
    own.wait()

    def across(d):
        block = w_ref.at[row, :, xy]
        return pltpu.make_async_remote_copy(
            block, block, ssem.at[d], rsem.at[d], device_id=plane(d), device_id_type=MESH
        )

    def arrive(d):
        m = lax.rem(me + 32 - d, 32)
        block = w_ref.at[lax.rem(m, 4), :, m // 4]
        return pltpu.make_async_remote_copy(
            block, block, ssem.at[d], rsem.at[d], device_id=plane(d), device_id_type=MESH
        )

    def go(d, c):
        across(d).start()
        return c

    lax.fori_loop(1, 32, go, 0)

    def done(d, c):
        across(d).wait_send()
        arrive(d).wait_recv()
        return c

    lax.fori_loop(1, 32, done, 0)


@functools.lru_cache(maxsize=None)
def sample_plan(rows_dev):
    yy = ((np.arange(NPIX) + 0.5) / NPIX * 2.0 - 1.0)[:, None]
    xx = ((np.arange(NPIX) + 0.5) / NPIX * 2.0 - 1.0)[None, :]
    u = (np.sqrt(xx * xx + yy * yy) - R_INNER) / (1.0 - R_INNER) * NR - 0.5
    v = (np.arctan2(yy, xx) + np.pi) / (2.0 * np.pi) * NPHI - 0.5
    blocks = NPIX // rows_dev
    plans = []
    for b in range(blocks):
        plan = []
        for c in range(NPIX // 128):
            cut = np.s_[b * rows_dev : (b + 1) * rows_dev, c * 128 : (c + 1) * 128]
            uu, vv = u[cut], v[cut]
            for q in range(NR // 128):
                hit = (uu > q * 128 - 1.01) & (uu < q * 128 + 128.01)
                if hit.any():
                    lo = int(np.floor((vv[hit].min() - 0.01) / 8))
                    hi = int(np.floor((np.floor(vv[hit].max() + 0.01) + 1) / 8))
                    plan.append((c, q, lo, hi - lo + 1))
        plans.append(plan)
    most = max(len(p) for p in plans)
    table = np.zeros((blocks, most, 4), np.int32)
    for b, plan in enumerate(plans):
        table[b, : len(plan)] = plan
    return table


def geometry(first_row, rows_dev):
    rows = first_row + jnp.arange(rows_dev, dtype=jnp.int32)
    yy = ((rows.astype(F32) + 0.5) / NPIX * 2.0 - 1.0)[:, None]
    xx = ((jnp.arange(NPIX, dtype=jnp.int32).astype(F32) + 0.5) / NPIX * 2.0 - 1.0)[None, :]
    dist = jnp.sqrt(xx * xx + yy * yy)
    upos = (dist - R_INNER) / (1.0 - R_INNER) * NR - 0.5
    vpos = (jnp.arctan2(yy, xx) + jnp.pi) / (2.0 * jnp.pi) * NPHI - 0.5
    return jnp.concatenate([upos, upos], axis=0), jnp.concatenate([vpos, vpos], axis=0)


def sample_kernel(plan_ref, u_ref, v_ref, w_ref, out_ref, acc, *, most):
    acc[...] = jnp.zeros_like(acc)
    sub = lax.broadcasted_iota(jnp.int32, (8, 128), 0)

    def task(t, carry):
        chunk, q, lo, count = (plan_ref[t, i] for i in range(4))
        cols = pl.ds(pl.multiple_of(chunk * 128, 128), 128)
        u, v = u_ref[:, cols], v_ref[:, cols]
        floor = jnp.floor(u)
        part = u - floor
        k = floor.astype(jnp.int32) - q * 128 + jnp.where(sub >= 4, 1, 0)
        weight = jnp.where(sub >= 4, part, 1.0 - part)
        weight = jnp.where((k >= 0) & (k < 128), weight, 0.0)
        k = jnp.clip(k, 0, 127)

        def tiles(i, total):
            base = (lo + i) * 8
            start = pl.multiple_of(lax.rem(base + NPHI, NPHI), 8)
            block = w_ref[q, pl.ds(start, 8), :]
            shifted = v - base.astype(F32)
            for s in range(8):
                row = jnp.broadcast_to(block[s : s + 1, :], (8, 128))
                got = jnp.take_along_axis(row, k, axis=1, mode="promise_in_bounds")
                total = total + jnp.maximum(1.0 - jnp.abs(shifted - float(s)), 0.0) * got
            return total

        total = lax.fori_loop(0, count, tiles, jnp.zeros((8, 128), F32))
        acc[:, cols] = acc[:, cols] + weight * total
        return carry

    lax.fori_loop(0, most, task, 0)
    out_ref[...] = acc[0:4, :] + acc[4:8, :]


def body(density, velocity, shifts, fractions):
    phi, row = lax.axis_index("phi"), lax.axis_index("row")
    z, x, y = phi // 8, (phi // 2) % 4, phi % 2
    local = z + 8 * y
    band = row * 16 + local
    shift = lax.dynamic_index_in_dim(shifts, local, keepdims=False)
    frac = lax.dynamic_slice_in_dim(fractions, local, 1)
    flag = lambda c: c.astype(jnp.int32)
    ints = jnp.stack([shift // 16, shift % 16, flag(band > 0), flag(band < 63), flag(x > 0), flag(x < 3)])
    ends = jnp.stack([flag(row > 0), flag(row < 3)])
    sds = lambda *s: jax.ShapeDtypeStruct(s, F32)

    tiles, edge = pl.pallas_call(
        to_tiles_kernel, name="to_tiles", out_shape=(sds(4, 4, 128, 128), sds(2, 16, 128)),
        in_specs=[VM, VM], out_specs=(VM, VM),
    )(density, velocity)
    hphi, hr = pl.pallas_call(
        first_edges_kernel, name="edges_a", out_shape=(sds(2, 4, 32, 128), sds(2, 16, 128)),
        in_specs=[ANY, ANY, ANY], out_specs=(ANY, ANY),
        scratch_shapes=[pltpu.SemaphoreType.DMA((6,)), pltpu.SemaphoreType.DMA((6,))],
        compiler_params=pltpu.CompilerParams(collective_id=0, has_side_effects=True),
    )(density, velocity, edge)
    stepped = pl.pallas_call(
        first_hydro_kernel, name="hydro_a", out_shape=sds(64, 4, 8, 128),
        in_specs=[SM, VM, VM, VM], out_specs=VM,
        scratch_shapes=[pltpu.VMEM((4, 4, 144, 128), F32), pltpu.VMEM((2, 128, 128), F32)],
    )(ends, tiles, hphi, hr)
    cyc = all_to_all(stepped, 1)
    moved, th_edge, r_edge = pl.pallas_call(
        first_advect_kernel, name="advect_a",
        out_shape=(sds(64, 4, 8, 128), sds(2, 8, 4, 8, 128), sds(2, 64, 4, 128)),
        in_specs=[SM, SM, VM], out_specs=(VM, VM, VM),
    )(ints, frac, cyc)
    hth, hr2 = pl.pallas_call(
        second_edges_kernel, name="edges_b", out_shape=(sds(2, 8, 4, 8, 128), sds(2, 64, 4, 128)),
        in_specs=[ANY, ANY], out_specs=(ANY, ANY),
        scratch_shapes=[pltpu.SemaphoreType.DMA((4,)), pltpu.SemaphoreType.DMA((4,))],
        compiler_params=pltpu.CompilerParams(collective_id=2, has_side_effects=True),
    )(th_edge, r_edge)
    final = pl.pallas_call(
        second_hydro_kernel, name="hydro_b", out_shape=sds(64, 4, 8, 128),
        in_specs=[SM, SM, VM, VM, VM], out_specs=VM,
        scratch_shapes=[pltpu.VMEM((64, 4, 8, 128), F32)],
    )(ints, frac, moved, hth, hr2)
    back = all_to_all(final, 3)
    rho, vel, light = pl.pallas_call(
        from_tiles_kernel, name="from_tiles", out_shape=(sds(16, 32, 128), sds(3, 16, 32, 128), sds(16, 128)),
        in_specs=[SM, VM], out_specs=(VM, VM, VM),
        scratch_shapes=[pltpu.VMEM((512, 128), F32)],
    )(jnp.reshape(row, (1,)), back)
    table = pl.pallas_call(
        gather_kernel, name="gather", out_shape=sds(4, 8, 8, 16, 128),
        in_specs=[ANY], out_specs=ANY,
        scratch_shapes=[pltpu.SemaphoreType.DMA((40,)), pltpu.SemaphoreType.DMA((40,)), pltpu.SemaphoreType.DMA],
        compiler_params=pltpu.CompilerParams(collective_id=4, has_side_effects=True),
    )(light)
    rows_dev = 4
    spot = phi * 4 + row
    plan = sample_plan(rows_dev)
    upos, vpos = geometry(spot * rows_dev, rows_dev)
    image = pl.pallas_call(
        functools.partial(sample_kernel, most=plan.shape[1]), name="sample", out_shape=sds(4, 1024),
        in_specs=[SM, VM, VM, VM], out_specs=VM,
        scratch_shapes=[pltpu.VMEM((8, 1024), F32)],
    )(lax.dynamic_index_in_dim(jnp.asarray(plan), spot, keepdims=False), upos, vpos, table.reshape(4, 1024, 128))
    return rho, vel, image


def solution(mesh):
    in_specs = (P("phi", None, "row"), P(None, "phi", None, "row"), P("row"), P("row"))
    out_specs = (P("phi", None, "row"), P(None, "phi", None, "row"), P(("phi", "row"), None))
    return jax.shard_map(body, mesh=mesh, in_specs=in_specs, out_specs=out_specs, check_vma=False)
```

```python
import functools

import jax
import jax.numpy as jnp
import numpy as np
from jax import lax
from jax.experimental import pallas as pl
from jax.experimental.pallas import tpu as pltpu
from jax.sharding import PartitionSpec as P

MESH = pl.DeviceIdType.MESH
BAND = 8
NPIX = 1024
NPHI = 1024
NR = 512
NTH = 32
KAPPA = 1.5
R_INNER = 0.2
F32 = jnp.float32
VM = pl.BlockSpec(memory_space=pltpu.VMEM)
SM = pl.BlockSpec(memory_space=pltpu.SMEM)
ANY = pl.BlockSpec(memory_space=pl.ANY)


def where_of(band, group):
    return (band % 8) * 8 + group * 2 + band // 8


def lanes():
    return lax.broadcasted_iota(jnp.int32, (8, 128), 1)


def conserved(q):
    return [q[0], q[0] * q[1], q[0] * q[2], q[0] * q[3]]


def side(q, comp, offset):
    m = q[0] * (0.5 * q[comp] + offset)
    out = [m, m * q[1], m * q[2], m * q[3]]
    out[comp] = out[comp] + 0.5 * q[0]
    return out


def updated(here, lower, upper):
    total = None
    for (comp, low), (_, high) in zip(lower, upper):
        p, m = side(low, comp, 0.75), side(high, comp, -0.75)
        part = [b - a for a, b in zip(p, m)]
        total = part if total is None else [s + t for s, t in zip(total, part)]
    new = [0.775 * c - 0.05 * t for c, t in zip(conserved(here), total)]
    inv = 1.0 / new[0]
    return [new[0], new[1] * inv, new[2] * inv, new[3] * inv]


def spread(i):
    return jnp.where(i % 2 == 0, 4 + i // 2, 4 - (i + 1) // 2)


def position():
    phi, row = lax.axis_index("phi"), lax.axis_index("row")
    return phi, row, phi // 8, lax.rem(phi // 2, 4), lax.rem(phi, 2)


def signal(peer):
    pl.semaphore_signal(pltpu.get_barrier_semaphore(), inc=1, device_id=peer, device_id_type=MESH)


def signal_cycle(phi):
    def sig(d, c):
        signal({"phi": lax.rem(phi + d, 64)})
        return c

    lax.fori_loop(1, 64, sig, 0)


def remote(src, dst, ssem, rsem, to):
    return pltpu.make_async_remote_copy(src, dst, ssem, rsem, device_id=to, device_id_type=MESH)


def first_kernel(rho_ref, vel_ref, out_ref, pad, edge, hphi, hr, ht, stepped, essem, ersem, ssem, rsem, lsem):
    phi, row, z, _, _ = position()
    left, right = {"phi": lax.rem(phi + 63, 64)}, {"phi": lax.rem(phi + 1, 64)}
    below, above = {"row": lax.rem(row + 3, 4)}, {"row": lax.rem(row + 1, 4)}
    signal_cycle(phi)
    signal(below)
    signal(above)
    for f in range(4):
        for g in range(4):
            src = rho_ref[:, 8 * g : 8 * g + 8, :] if f == 0 else vel_ref[f - 1, :, 8 * g : 8 * g + 8, :]
            t = src.reshape(128, 128).T
            pad[f, g, 8:136, :] = t
            edge[0, pl.ds(f * 4 + g, 1), :] = t[0:1, :]
            edge[1, pl.ds(f * 4 + g, 1), :] = t[127:128, :]
    pl.semaphore_wait(pltpu.get_barrier_semaphore(), 65)
    copies = [
        remote(rho_ref.at[15], hphi.at[0, 0], essem.at[0], ersem.at[0], right),
        remote(vel_ref.at[:, 15], hphi.at[0, pl.ds(1, 3)], essem.at[1], ersem.at[1], right),
        remote(rho_ref.at[0], hphi.at[1, 0], essem.at[2], ersem.at[2], left),
        remote(vel_ref.at[:, 0], hphi.at[1, pl.ds(1, 3)], essem.at[3], ersem.at[3], left),
        remote(edge.at[1], hr.at[0], essem.at[4], ersem.at[4], above),
        remote(edge.at[0], hr.at[1], essem.at[5], ersem.at[5], below),
    ]
    for c in copies:
        c.start()
    for c in copies:
        c.wait()
    has_low = jnp.where(row > 0, 1.0, 0.0)
    has_high = jnp.where(row < 3, 1.0, 0.0)
    for pair in range(2):
        ht[pair] = jnp.concatenate([hphi[s, 2 * pair + f] for f in range(2) for s in range(2)], axis=0).T
    for f in range(4):
        for g in range(4):
            pad[f, g, 7:8, :] = hr[0, pl.ds(f * 4 + g, 1), :] * has_low
            pad[f, g, 136:137, :] = hr[1, pl.ds(f * 4 + g, 1), :] * has_high
    lane = lanes()
    first, last = lane < 8, lane >= 120
    low_th, high_th = (lane % 8) == 0, (lane % 8) == 7

    def band_at(i):
        return lax.rem(z + spread(i // 2), 8) + 8 * (i % 2)

    def spot(i, g):
        j = band_at(i)
        return lax.rem(j, 8) * 8 + g * 2 + j // 8

    def message(d):
        off = lax.rem(d - phi + 64, 64)
        return remote(stepped.at[d], out_ref.at[phi], ssem.at[off], rsem.at[off], {"phi": d})

    own = pltpu.make_async_copy(stepped.at[phi], out_ref.at[phi], lsem)

    def send(i):
        for g in range(4):
            d = spot(i, g)

            @pl.when(d != phi)
            def _():
                message(d).start()

            @pl.when(d == phi)
            def _():
                own.start()

    def step(i, carry):
        j = band_at(i)
        base = pl.multiple_of(8 * j, 8)
        here = [[pad[f, g, pl.ds(base + 8, 8), :] for f in range(4)] for g in range(4)]
        side_edge = [ht[pair, pl.ds(base, 8), :] for pair in range(2)]
        for g in range(4):
            c = here[g]
            before = [pad[f, g, pl.ds(base, 16), :][7:15] for f in range(4)]
            after = [pad[f, g, pl.ds(base + 8, 16), :][1:9] for f in range(4)]
            thm, thp, phm, php = [], [], [], []
            for f in range(4):
                lo = pltpu.roll(here[g - 1][f], 121, 1) if g > 0 else jnp.zeros((8, 128), F32)
                hi = pltpu.roll(here[g + 1][f], 7, 1) if g < 3 else jnp.zeros((8, 128), F32)
                thm.append(jnp.where(low_th, lo, pltpu.roll(c[f], 1, 1)))
                thp.append(jnp.where(high_th, hi, pltpu.roll(c[f], 127, 1)))
                off = (f % 2) * 64 + g * 8
                lo = pltpu.roll(side_edge[f // 2], (128 - off) % 128, 1)
                hi = pltpu.roll(side_edge[f // 2], (120 - off - 32) % 128, 1)
                phm.append(jnp.where(first, lo, pltpu.roll(c[f], 8, 1)))
                php.append(jnp.where(last, hi, pltpu.roll(c[f], 120, 1)))
            new = updated(c, ((2, phm), (3, thm), (1, before)), ((2, php), (3, thp), (1, after)))
            d = spot(i, g)
            for f in range(4):
                stepped[d, f] = new[f]

        @pl.when(i > 0)
        def _():
            send(i - 1)

        return carry

    lax.fori_loop(0, 16, step, 0)
    send(15)

    def done(off, c):
        message(lax.rem(phi + off, 64)).wait()
        return c

    lax.fori_loop(1, 64, done, 0)
    own.wait()


def second_kernel(
    shift_ref, frac_ref, cyc, back, table, rho_back,
    t1, th_edge, r_edge, hth, hr, fin, flat, light,
    essem, ersem, rs, rr, vs, vr, ls, us, ur, ps, prs, ss, sr, hs, hrs,
):
    phi, row, z, x, y = position()
    half, zl, xy = z // 4, lax.rem(z, 4), lax.rem(phi, 8)
    core, yh = lax.rem(row, 2), row // 2
    band = row * 16 + y * 8 + z

    def at_band(b):
        j = lax.rem(b, 16)
        return {"phi": lax.rem(j, 8) * 8 + x * 2 + j // 8, "row": b // 16}

    def at_group(g):
        return {"phi": z * 8 + g * 2 + y}

    def chip(n):
        m = lax.rem(xy * 2 + yh + n, 16)
        return {"phi": z * 8 + m // 2, "row": lax.rem(m, 2) * 2 + core}

    sibling = {"row": yh * 2 + 1 - core}
    below, above = at_band(lax.rem(band + 63, 64)), at_band(lax.rem(band + 1, 64))
    left, right = at_group(lax.rem(x + 3, 4)), at_group(lax.rem(x + 1, 4))
    signal_cycle(phi)
    for peer in (below, above, sibling):
        signal(peer)
    for n in range(1, 16):
        signal(chip(n))

    local = z + 8 * y
    shift = shift_ref[local]
    w = frac_ref[local]
    whole, remain = shift // 16, shift % 16
    lane = lanes()
    lane8 = lane % 8
    one, two = 8 * remain, 8 * (remain + 1)
    two_roll = lax.rem(two, 128)
    keep_one, keep_two = lane >= one, lane >= two

    def turn(tiles):
        return [pltpu.roll(t, one, 1) for t in tiles] + [pltpu.roll(t, two_roll, 1) for t in tiles]

    def blend(cur, prev):
        out = []
        for f in range(4):
            lead = jnp.where(keep_one, cur[f], prev[f])
            trail = jnp.where(keep_two, cur[4 + f], prev[4 + f])
            out.append((1.0 - w) * lead + w * trail)
        return out

    def cycle_slab(p):
        slab = lax.rem(p + 128 - whole, 64)
        return turn([cyc[slab, f] for f in range(4)])

    def move(big, prev):
        top, bottom = [None] * 4, [None] * 4
        for j in range(8):
            cur = cycle_slab(big * 8 + j)
            out = blend(cur, prev)
            prev = cur
            for f in range(4):
                t = out[f]
                t1[big * 8 + j, f] = t
                hi = pltpu.roll(t, (j - 7) % 128, 1)
                lo = pltpu.roll(t, j, 1)
                top[f] = hi if j == 0 else jnp.where(lane8 == j, hi, top[f])
                bottom[f] = lo if j == 0 else jnp.where(lane8 == j, lo, bottom[f])
                r_edge[0, big * 8 + j, pl.ds(f, 1), :] = t[0:1, :]
                r_edge[1, big * 8 + j, pl.ds(f, 1), :] = t[7:8, :]
        for f in range(4):
            th_edge[0, big, f] = bottom[f]
            th_edge[1, big, f] = top[f]
        return prev

    lax.fori_loop(0, 8, move, cycle_slab(-1))

    pl.semaphore_wait(pltpu.get_barrier_semaphore(), 81)
    copies = [
        remote(r_edge.at[1], hr.at[0], essem.at[0], ersem.at[0], above),
        remote(r_edge.at[0], hr.at[1], essem.at[1], ersem.at[1], below),
        remote(th_edge.at[1], hth.at[0], essem.at[2], ersem.at[2], right),
        remote(th_edge.at[0], hth.at[1], essem.at[3], ersem.at[3], left),
    ]
    for c in copies:
        c.start()
    for c in copies:
        c.wait()

    on = [jnp.where(c, 1.0, 0.0) for c in (band > 0, band < 63, x > 0, x < 3)]
    sub = lax.broadcasted_iota(jnp.int32, (8, 128), 0)
    first, last = lane < 8, lane >= 120
    low_th, high_th = lane8 == 0, lane8 == 7
    low_r, high_r = sub == 0, sub == 7

    def hydro_slab(p):
        q = lax.rem(p + 128 - whole, 64)
        before, after = lax.rem(q + 63, 64), lax.rem(q + 1, 64)
        big, j = q // 8, lax.rem(q, 8)
        back_by = lax.rem(128 - j, 128)
        c = [t1[q, f] for f in range(4)]
        thm, thp, phm, php, rm, rp = [], [], [], [], [], []
        for f in range(4):
            thm.append(jnp.where(low_th, pltpu.roll(hth[0, big, f] * on[2], back_by, 1), pltpu.roll(c[f], 1, 1)))
            thp.append(jnp.where(high_th, pltpu.roll(hth[1, big, f] * on[3], 7 - j, 1), pltpu.roll(c[f], 127, 1)))
            phm.append(jnp.where(first, pltpu.roll(t1[before, f], 8, 1), pltpu.roll(c[f], 8, 1)))
            php.append(jnp.where(last, pltpu.roll(t1[after, f], 120, 1), pltpu.roll(c[f], 120, 1)))
            lo = hr[0, q, pl.ds(f, 1), :] * on[0]
            hi = hr[1, q, pl.ds(f, 1), :] * on[1]
            rm.append(jnp.where(low_r, jnp.broadcast_to(lo, (8, 128)), pltpu.roll(c[f], 1, 0)))
            rp.append(jnp.where(high_r, jnp.broadcast_to(hi, (8, 128)), pltpu.roll(c[f], 7, 0)))
        new = updated(c, ((2, phm), (3, thm), (1, rm)), ((2, php), (3, thp), (1, rp)))
        return turn(new)

    def rho_message(p):
        off = lax.rem(p - phi + 64, 64)
        return remote(fin.at[p, 0], rho_back.at[phi], rs.at[off], rr.at[off], {"phi": p})

    def vel_message(p):
        off = lax.rem(p - phi + 64, 64)
        return remote(fin.at[p, pl.ds(1, 3)], back.at[phi], vs.at[off], vr.at[off], {"phi": p})

    own_rho = pltpu.make_async_copy(fin.at[phi, 0], rho_back.at[phi], ls.at[0])
    own_vel = pltpu.make_async_copy(fin.at[phi, pl.ds(1, 3)], back.at[phi], ls.at[1])

    def send(zoff, message, own):
        def one_slab(i, c):
            p = lax.rem(z + zoff, 8) * 8 + i

            @pl.when(p != phi)
            def _():
                message(p).start()

            @pl.when(p == phi)
            def _():
                own.start()

            return c

        lax.fori_loop(0, 8, one_slab, 0)

    def block(i, carry):
        start = lax.rem(z + spread(i), 8) * 8

        def slab(k, prev):
            cur = hydro_slab(start + k)
            out = blend(cur, prev)
            for f in range(4):
                fin[start + k, f] = out[f]
            return cur

        lax.fori_loop(0, 8, slab, hydro_slab(start - 1))

        @pl.when(i > 0)
        def _():
            send(spread(i - 1), rho_message, own_rho)

        return carry

    lax.fori_loop(0, 8, block, 0)
    send(0, rho_message, own_rho)
    send(4, vel_message, own_vel)

    def rho_done(off, c):
        rho_message(lax.rem(phi + off, 64)).wait()
        return c

    lax.fori_loop(1, 64, rho_done, 0)
    own_rho.wait()
    for g in range(4):
        t = jnp.concatenate([rho_back[where_of(j, g)] for j in range(16)], axis=0).T.reshape(16, 8, 128)
        for i in range(16):
            flat[pl.ds(i * 32 + 8 * g, 8), :] = t[i]
    k = row * 128 + lax.broadcasted_iota(jnp.int32, (16, 128), 1)
    radius = R_INNER + (k.astype(F32) + 0.5) * (1.0 - R_INNER) / NR
    seen = jnp.ones((16, 128), F32)
    total = jnp.zeros((16, 128), F32)
    for j in range(NTH):
        tilt = float(np.float32(1.0 + 0.5 * np.cos(np.pi * (j + 0.5) / NTH)))
        t = jnp.exp(flat[pl.ds(j, 16, stride=32), :] * (-KAPPA / NTH))
        total = total + tilt * ((1.0 - t) * seen)
        seen = seen * t
    light[...] = (1.0 / jnp.sqrt(radius)) * total

    slot = zl * 8 + xy + 1
    own_light = pltpu.make_async_copy(light, table.at[row, slot], ls.at[2])
    own_light.start()

    def up(n, far, dst):
        return remote(
            light, table.at[row, dst], us.at[far * 4 + n], ur.at[far * 4 + n],
            {"phi": ((half + far) % 2 * 4 + lax.rem(zl + n, 4)) * 8 + xy},
        )

    low_end, high_end = (xy == 0) & (zl == 0), (xy == 7) & (zl == 3)
    for n in range(1, 4):
        up(n, 0, slot).start()
    for cond, dst in ((low_end, 33), (high_end, 0)):

        @pl.when(cond)
        def _(dst=dst):
            for n in range(4):
                up(n, 1, dst).start()

    send(3, vel_message, own_vel)
    send(5, vel_message, own_vel)
    for n in range(1, 4):
        up(n, 0, slot).wait()
    own_light.wait()
    for end, cond, dst in ((0, low_end, 33), (3, high_end, 0)):

        @pl.when(cond)
        def _(dst=dst):
            for n in range(4):
                up(n, 1, dst).wait_send()

        for pos in range(4):

            @pl.when((xy == (0 if end == 0 else 7)) & (zl == pos))
            def _(pos=pos, end=end, dst=dst):
                up((pos - end) % 4, 1, dst).wait_recv()

    def main_copy(q, pos, ssem, rsem, to):
        return [
            remote(table.at[q, 1 + 8 * b + pos], table.at[q, 1 + 8 * b + pos], ssem.at[b], rsem.at[b], to)
            for b in range(4)
        ]

    def end_copy(q, dst, ssem, rsem, to):
        return remote(table.at[q, dst], table.at[q, dst], ssem, rsem, to)

    def to_chip(n, c):
        to = chip(n)
        for cp in main_copy(row, xy, ps.at[n], prs.at[n], to):
            cp.start()
        for pos, dst in ((0, 33), (7, 0)):

            @pl.when(xy == pos)
            def _(dst=dst):
                end_copy(row, dst, hs.at[n], hrs.at[n], to).start()

        return c

    def give(q, pos, n):
        for cp in main_copy(q, pos, ss.at[n], sr.at[n], sibling):
            cp.start()
        for at, dst in ((0, 33), (7, 0)):

            @pl.when(pos == at)
            def _(dst=dst):
                end_copy(q, dst, hs.at[16 + n], hrs.at[16 + n], sibling).start()

    lax.fori_loop(1, 16, to_chip, 0)
    give(row, xy, 0)
    for off in (2, 6, 1, 7, 0):
        send(off, vel_message, own_vel)

    def source(n):
        m = lax.rem(xy * 2 + yh + 16 - n, 16)
        return m // 2, lax.rem(m, 2)

    def from_chip(n, c):
        pos, high = source(n)
        q = high * 2 + core
        for cp in main_copy(q, pos, ps.at[n], prs.at[n], chip(n)):
            cp.wait_recv()
        for at, dst in ((0, 33), (7, 0)):

            @pl.when(pos == at)
            def _(dst=dst):
                end_copy(q, dst, hs.at[n], hrs.at[n], chip(n)).wait_recv()

        give(q, pos, n)
        return c

    lax.fori_loop(1, 16, from_chip, 0)

    def finish(n, c):
        pos, high = source(n)
        q = high * 2 + core
        other = high * 2 + 1 - core
        for cp in main_copy(q, pos, ss.at[n], sr.at[n], sibling):
            cp.wait_send()
        for cp in main_copy(other, pos, ss.at[n], sr.at[n], sibling):
            cp.wait_recv()
        for at, dst in ((0, 33), (7, 0)):

            @pl.when(pos == at)
            def _(dst=dst):
                end_copy(q, dst, hs.at[16 + n], hrs.at[16 + n], sibling).wait_send()
                end_copy(other, dst, hs.at[16 + n], hrs.at[16 + n], sibling).wait_recv()

        return c

    lax.fori_loop(0, 16, finish, 0)

    def sent(n, c):
        for cp in main_copy(row, xy, ps.at[n], prs.at[n], chip(n)):
            cp.wait_send()
        for at, dst in ((0, 33), (7, 0)):

            @pl.when(xy == at)
            def _(dst=dst):
                end_copy(row, dst, hs.at[n], hrs.at[n], chip(n)).wait_send()

        return c

    lax.fori_loop(1, 16, sent, 0)

    def vel_done(off, c):
        vel_message(lax.rem(phi + off, 64)).wait()
        return c

    lax.fori_loop(1, 64, vel_done, 0)
    own_vel.wait()


@functools.lru_cache(maxsize=None)
def sample_plan(rows_dev):
    yy = ((np.arange(NPIX) + 0.5) / NPIX * 2.0 - 1.0)[:, None]
    xx = ((np.arange(NPIX) + 0.5) / NPIX * 2.0 - 1.0)[None, :]
    u = (np.sqrt(xx * xx + yy * yy) - R_INNER) / (1.0 - R_INNER) * NR - 0.5
    v = (np.arctan2(yy, xx) + np.pi) / (2.0 * np.pi) * NPHI - 0.5
    blocks = NPIX // rows_dev
    plans = []
    for b in range(blocks):
        plan = []
        for c in range(NPIX // 128):
            cut = np.s_[b * rows_dev : (b + 1) * rows_dev, c * 128 : (c + 1) * 128]
            uu, vv = u[cut], v[cut]
            for q in range(NR // 128):
                hit = (uu > q * 128 - 1.01) & (uu < q * 128 + 128.01)
                if hit.any():
                    lo = int(np.floor((vv[hit].min() - 0.01) / 8))
                    hi = int(np.floor((np.floor(vv[hit].max() + 0.01) + 1) / 8))
                    plan.append((c, q, lo, hi - lo + 1))
        plans.append(plan)
    most = max(len(p) for p in plans)
    table = np.zeros((blocks, most, 4), np.int32)
    for b, plan in enumerate(plans):
        table[b, : len(plan)] = plan
    return table


def last_kernel(plan_ref, u_ref, v_ref, rho_src, vel_src, w_ref, rho_ref, vel_ref, out_ref, acc, *, most):
    phi, row = lax.axis_index("phi"), lax.axis_index("row")
    for f in range(4):
        for g in range(4):
            x = jnp.concatenate(
                [rho_src[where_of(j, g)] if f == 0 else vel_src[where_of(j, g), f - 1] for j in range(16)], axis=0
            )
            t = x.T.reshape(16, 8, 128)
            if f == 0:
                rho_ref[:, 8 * g : 8 * g + 8, :] = t
            else:
                vel_ref[f - 1, :, 8 * g : 8 * g + 8, :] = t
    spot = phi * 4 + row
    first_tile = phi // 32 * 64 - 2
    acc[...] = jnp.zeros_like(acc)
    sub = lax.broadcasted_iota(jnp.int32, (8, 128), 0)

    def task(t, carry):
        word = plan_ref[spot * most + t]
        chunk, q = word % 8, word // 8 % 4
        lo, count = word // 32 % 256 - 1, word // 8192
        cols = pl.ds(pl.multiple_of(chunk * 128, 128), 128)
        u, v = u_ref[:, cols], v_ref[:, cols]
        floor = jnp.floor(u)
        part = u - floor
        k = floor.astype(jnp.int32) - q * 128 + jnp.where(sub >= 4, 1, 0)
        weight = jnp.where(sub >= 4, part, 1.0 - part)
        weight = jnp.where((k >= 0) & (k < 128), weight, 0.0)
        k = jnp.clip(k, 0, 127)

        def tiles(i, total):
            base = (lo + i) * 8
            start = pl.multiple_of((lo + i - first_tile) * 8, 8)
            block = w_ref[q, pl.ds(start, 8), :]
            shifted = v - base.astype(F32)
            for s in range(8):
                line = jnp.broadcast_to(block[s : s + 1, :], (8, 128))
                got = jnp.take_along_axis(line, k, axis=1, mode="promise_in_bounds")
                total = total + jnp.maximum(1.0 - jnp.abs(shifted - float(s)), 0.0) * got
            return total

        total = lax.fori_loop(0, count, tiles, jnp.zeros((8, 128), F32))
        acc[:, cols] = acc[:, cols] + weight * total
        return carry

    lax.fori_loop(0, most, task, 0)
    out_ref[...] = acc[0:4, :] + acc[4:8, :]


def geometry(first_row, rows_dev):
    rows = first_row + jnp.arange(rows_dev, dtype=jnp.int32)
    yy = ((rows.astype(F32) + 0.5) / NPIX * 2.0 - 1.0)[:, None]
    xx = ((jnp.arange(NPIX, dtype=jnp.int32).astype(F32) + 0.5) / NPIX * 2.0 - 1.0)[None, :]
    dist = jnp.sqrt(xx * xx + yy * yy)
    upos = (dist - R_INNER) / (1.0 - R_INNER) * NR - 0.5
    vpos = (jnp.arctan2(yy, xx) + jnp.pi) / (2.0 * jnp.pi) * NPHI - 0.5
    return jnp.concatenate([upos, upos], axis=0), jnp.concatenate([vpos, vpos], axis=0)


def body(density, velocity, shifts, fractions):
    phi, row = lax.axis_index("phi"), lax.axis_index("row")
    sds = lambda *s: jax.ShapeDtypeStruct(s, F32)
    dma = lambda *s: pltpu.SemaphoreType.DMA(s)
    vmem = lambda *s: pltpu.VMEM(s, F32)
    cyc = pl.pallas_call(
        first_kernel, name="first", out_shape=sds(64, 4, 8, 128),
        in_specs=[VM, VM], out_specs=ANY,
        scratch_shapes=[
            vmem(4, 4, 144, 128), vmem(2, 16, 128), vmem(2, 4, 32, 128), vmem(2, 16, 128), vmem(2, 128, 128),
            vmem(64, 4, 8, 128), dma(6), dma(6), dma(64), dma(64), pltpu.SemaphoreType.DMA,
        ],
        compiler_params=pltpu.CompilerParams(collective_id=0, has_side_effects=True),
    )(density, velocity)
    back, table, rho_back = pl.pallas_call(
        second_kernel, name="second", out_shape=(sds(64, 3, 8, 128), sds(4, 34, 16, 128), sds(64, 8, 128)),
        in_specs=[SM, SM, VM], out_specs=(ANY, ANY, VM),
        scratch_shapes=[
            vmem(64, 4, 8, 128), vmem(2, 8, 4, 8, 128), vmem(2, 64, 4, 128), vmem(2, 8, 4, 8, 128), vmem(2, 64, 4, 128),
            vmem(64, 4, 8, 128), vmem(512, 128), vmem(16, 128),
            dma(4), dma(4), dma(64), dma(64), dma(64), dma(64), dma(3), dma(8), dma(8),
            dma(16, 4), dma(16, 4), dma(16, 4), dma(16, 4), dma(32), dma(32),
        ],
        compiler_params=pltpu.CompilerParams(collective_id=1, has_side_effects=True),
    )(shifts, fractions, cyc)
    plan = sample_plan(4)
    most = plan.shape[1]
    words = plan[..., 0] + 8 * plan[..., 1] + 32 * (plan[..., 2] + 1) + 8192 * plan[..., 3]
    upos, vpos = geometry((phi * 4 + row) * 4, 4)
    return pl.pallas_call(
        functools.partial(last_kernel, most=most), name="last",
        out_shape=(sds(16, 32, 128), sds(3, 16, 32, 128), sds(4, 1024)),
        in_specs=[SM, VM, VM, VM, VM, VM], out_specs=(VM, VM, VM),
        scratch_shapes=[pltpu.VMEM((8, 1024), F32)],
    )(jnp.asarray(words.reshape(-1)), upos, vpos, rho_back, back, table.reshape(4, 544, 128))


def solution(mesh):
    in_specs = (P("phi", None, "row"), P(None, "phi", None, "row"), P("row"), P("row"))
    out_specs = (P("phi", None, "row"), P(None, "phi", None, "row"), P(("phi", "row"), None))
    return jax.shard_map(body, mesh=mesh, in_specs=in_specs, out_specs=out_specs, check_vma=False)
```

```python
import functools

import jax
import jax.numpy as jnp
import numpy as np
from jax import lax
from jax.experimental import pallas as pl
from jax.experimental.pallas import tpu as pltpu
from jax.sharding import PartitionSpec as P

MESH = pl.DeviceIdType.MESH
BAND = 8
NPIX = 1024
NPHI = 1024
NR = 512
NTH = 32
UNROLL = 4
KAPPA = 1.5
R_INNER = 0.2
F32 = jnp.float32
VM = pl.BlockSpec(memory_space=pltpu.VMEM)
SM = pl.BlockSpec(memory_space=pltpu.SMEM)
ANY = pl.BlockSpec(memory_space=pl.ANY)


def where_of(band, group):
    return (band % 8) * 8 + group * 2 + band // 8


def lanes():
    return lax.broadcasted_iota(jnp.int32, (8, 128), 1)


def conserved(q):
    return [q[0], q[0] * q[1], q[0] * q[2], q[0] * q[3]]


def side(q, comp, offset):
    m = q[0] * (0.5 * q[comp] + offset)
    out = [m, m * q[1], m * q[2], m * q[3]]
    out[comp] = out[comp] + 0.5 * q[0]
    return out


def updated(here, lower, upper):
    total = None
    for (comp, low), (_, high) in zip(lower, upper):
        p, m = side(low, comp, 0.75), side(high, comp, -0.75)
        part = [b - a for a, b in zip(p, m)]
        total = part if total is None else [s + t for s, t in zip(total, part)]
    new = [0.775 * c - 0.05 * t for c, t in zip(conserved(here), total)]
    inv = 1.0 / new[0]
    return [new[0], new[1] * inv, new[2] * inv, new[3] * inv]


def spread(i):
    return jnp.where(i % 2 == 0, 4 + i // 2, 4 - (i + 1) // 2)


def signal(peer):
    pl.semaphore_signal(pltpu.get_barrier_semaphore(), inc=1, device_id=peer, device_id_type=MESH)


def remote(src, dst, ssem, rsem, to):
    return pltpu.make_async_remote_copy(src, dst, ssem, rsem, device_id=to, device_id_type=MESH)


def wait_all(ref, sems):
    for sem in sems:
        pltpu.make_async_copy(ref, ref, sem).wait()


def main_kernel(
    shift_ref, frac_ref, rho_ref, vel_ref, back, table, rho_back, u_ref, v_ref,
    pad, edge, hphi, hr, ht, stepped, cyc, t1, th_edge, r_edge, hth, hr2, fin, flat, light,
    es, er, as_, ar, bs, br, rs, rr, vs, vr, ls, us, ur, hs, hrr, ps, pr, gs, gr,
):
    phi, row = lax.axis_index("phi"), lax.axis_index("row")
    z, x, y = phi // 8, lax.rem(phi // 2, 4), lax.rem(phi, 2)
    half, zl, xy = z // 4, lax.rem(z, 4), lax.rem(phi, 8)
    core, yh = lax.rem(row, 2), row // 2
    band = row * 16 + y * 8 + z

    def at_band(b):
        j = lax.rem(b, 16)
        return {"phi": lax.rem(j, 8) * 8 + x * 2 + j // 8, "row": b // 16}

    def at_group(g):
        return {"phi": z * 8 + g * 2 + y}

    def chip(n):
        m = lax.rem(xy * 2 + yh + n, 16)
        return {"phi": z * 8 + m // 2, "row": lax.rem(m, 2) * 2 + core}

    sibling = {"row": yh * 2 + 1 - core}
    phi_low, phi_high = {"phi": lax.rem(phi + 63, 64)}, {"phi": lax.rem(phi + 1, 64)}
    row_low, row_high = {"row": lax.rem(row + 3, 4)}, {"row": lax.rem(row + 1, 4)}
    band_low, band_high = at_band(lax.rem(band + 63, 64)), at_band(lax.rem(band + 1, 64))
    group_low, group_high = at_group(lax.rem(x + 3, 4)), at_group(lax.rem(x + 1, 4))

    def greet_phi(d, c):
        signal({"phi": lax.rem(phi + d, 64)})
        return c

    def greet_chip(n, c):
        signal(chip(n))
        return c

    lax.fori_loop(1, 64, greet_phi, 0)
    for peer in (row_low, row_high, band_low, band_high, sibling):
        signal(peer)
    lax.fori_loop(1, 16, greet_chip, 0)

    for f in range(4):
        for g in range(4):
            src = rho_ref[:, 8 * g : 8 * g + 8, :] if f == 0 else vel_ref[f - 1, :, 8 * g : 8 * g + 8, :]
            t = src.reshape(128, 128).T
            pad[f, g, 8:136, :] = t
            edge[0, pl.ds(f * 4 + g, 1), :] = t[0:1, :]
            edge[1, pl.ds(f * 4 + g, 1), :] = t[127:128, :]
    pl.semaphore_wait(pltpu.get_barrier_semaphore(), 83)
    copies = [
        remote(rho_ref.at[15], hphi.at[0, 0], es.at[0], er.at[0], phi_high),
        remote(vel_ref.at[:, 15], hphi.at[0, pl.ds(1, 3)], es.at[1], er.at[1], phi_high),
        remote(rho_ref.at[0], hphi.at[1, 0], es.at[2], er.at[2], phi_low),
        remote(vel_ref.at[:, 0], hphi.at[1, pl.ds(1, 3)], es.at[3], er.at[3], phi_low),
        remote(edge.at[1], hr.at[0], es.at[4], er.at[4], row_high),
        remote(edge.at[0], hr.at[1], es.at[5], er.at[5], row_low),
    ]
    for c in copies:
        c.start()
    for c in copies:
        c.wait()
    has_low = jnp.where(row > 0, 1.0, 0.0)
    has_high = jnp.where(row < 3, 1.0, 0.0)
    for pair in range(2):
        ht[pair] = jnp.concatenate([hphi[s, 2 * pair + f] for f in range(2) for s in range(2)], axis=0).T
    for f in range(4):
        for g in range(4):
            pad[f, g, 7:8, :] = hr[0, pl.ds(f * 4 + g, 1), :] * has_low
            pad[f, g, 136:137, :] = hr[1, pl.ds(f * 4 + g, 1), :] * has_high

    lane = lanes()
    lane8 = lane % 8
    first, last = lane < 8, lane >= 120
    low_th, high_th = lane8 == 0, lane8 == 7
    zero = jnp.zeros((8, 128), F32)

    def band_at(i):
        return lax.rem(z + spread(i // 2), 8) + 8 * (i % 2)

    def spot(i, g):
        j = band_at(i)
        return lax.rem(j, 8) * 8 + g * 2 + j // 8

    own = pltpu.make_async_copy(stepped.at[phi], cyc.at[phi], ls.at[0])

    def send_tiles(i):
        for g in range(4):
            d = spot(i, g)

            @pl.when(d != phi)
            def _():
                remote(stepped.at[d], cyc.at[phi], as_, ar, {"phi": d}).start()

            @pl.when(d == phi)
            def _():
                own.start()

    def step(i, carry):
        base = pl.multiple_of(8 * band_at(i), 8)
        here = [[pad[f, g, pl.ds(base + 8, 8), :] for f in range(4)] for g in range(4)]
        side_edge = [ht[pair, pl.ds(base, 8), :] for pair in range(2)]
        for g in range(4):
            c = here[g]
            before = [pad[f, g, pl.ds(base, 16), :][7:15] for f in range(4)]
            after = [pad[f, g, pl.ds(base + 8, 16), :][1:9] for f in range(4)]
            thm, thp, phm, php = [], [], [], []
            for f in range(4):
                lo = pltpu.roll(here[g - 1][f], 121, 1) if g > 0 else zero
                hi = pltpu.roll(here[g + 1][f], 7, 1) if g < 3 else zero
                thm.append(jnp.where(low_th, lo, pltpu.roll(c[f], 1, 1)))
                thp.append(jnp.where(high_th, hi, pltpu.roll(c[f], 127, 1)))
                off = (f % 2) * 64 + g * 8
                lo = pltpu.roll(side_edge[f // 2], (128 - off) % 128, 1)
                hi = pltpu.roll(side_edge[f // 2], (120 - off - 32) % 128, 1)
                phm.append(jnp.where(first, lo, pltpu.roll(c[f], 8, 1)))
                php.append(jnp.where(last, hi, pltpu.roll(c[f], 120, 1)))
            new = updated(c, ((2, phm), (3, thm), (1, before)), ((2, php), (3, thp), (1, after)))
            d = spot(i, g)
            for f in range(4):
                stepped[d, f] = new[f]

        @pl.when(i > 0)
        def _():
            send_tiles(i - 1)

        return carry

    lax.fori_loop(0, 16, step, 0)
    send_tiles(15)

    local = z + 8 * y
    shift = shift_ref[local]
    w = frac_ref[local]
    whole, remain = shift // 16, shift % 16
    one, two = 8 * remain, 8 * (remain + 1)
    two_roll = lax.rem(two, 128)
    keep_one, keep_two = lane >= one, lane >= two

    def turn(tiles):
        return [pltpu.roll(t, one, 1) for t in tiles] + [pltpu.roll(t, two_roll, 1) for t in tiles]

    def blend(cur, prev):
        out = []
        for f in range(4):
            lead = jnp.where(keep_one, cur[f], prev[f])
            trail = jnp.where(keep_two, cur[4 + f], prev[4 + f])
            out.append((1.0 - w) * lead + w * trail)
        return out

    def cycle_slab(p):
        slab = lax.rem(p + 128 - whole, 64)
        return turn([cyc[slab, f] for f in range(4)])

    def move(big, prev):
        top, bottom = [None] * 4, [None] * 4
        for j in range(8):
            cur = cycle_slab(big * 8 + j)
            out = blend(cur, prev)
            prev = cur
            for f in range(4):
                t = out[f]
                t1[big * 8 + j, f] = t
                hi = pltpu.roll(t, (j - 7) % 128, 1)
                lo = pltpu.roll(t, j, 1)
                top[f] = hi if j == 0 else jnp.where(lane8 == j, hi, top[f])
                bottom[f] = lo if j == 0 else jnp.where(lane8 == j, lo, bottom[f])
                r_edge[0, big * 8 + j, pl.ds(f, 1), :] = t[0:1, :]
                r_edge[1, big * 8 + j, pl.ds(f, 1), :] = t[7:8, :]
        for f in range(4):
            th_edge[0, big, f] = bottom[f]
            th_edge[1, big, f] = top[f]
        return prev

    pixel = (phi * 4 + row) * 4 + lax.broadcasted_iota(jnp.int32, (8, 1024), 0) % 4
    column = lax.broadcasted_iota(jnp.int32, (8, 1024), 1)
    yy = (pixel.astype(F32) + 0.5) / NPIX * 2.0 - 1.0
    xx = (column.astype(F32) + 0.5) / NPIX * 2.0 - 1.0
    dist = jnp.sqrt(xx * xx + yy * yy)
    u_ref[...] = (dist - R_INNER) / (1.0 - R_INNER) * NR - 0.5
    v_ref[...] = (jnp.arctan2(yy, xx) + jnp.pi) / (2.0 * jnp.pi) * NPHI - 0.5

    wait_all(cyc.at[pl.ds(0, 63)], (as_, ar))
    own.wait()
    lax.fori_loop(0, 8, move, cycle_slab(-1))
    copies = [
        remote(r_edge.at[1], hr2.at[0], bs.at[0], br.at[0], band_high),
        remote(r_edge.at[0], hr2.at[1], bs.at[1], br.at[1], band_low),
        remote(th_edge.at[1], hth.at[0], bs.at[2], br.at[2], group_high),
        remote(th_edge.at[0], hth.at[1], bs.at[3], br.at[3], group_low),
    ]
    for c in copies:
        c.start()
    for c in copies:
        c.wait()
    for side_of, cond in enumerate((band > 0, band < 63)):
        hr2[side_of] = hr2[side_of] * jnp.where(cond, 1.0, 0.0)
    for side_of, cond in enumerate((x > 0, x < 3)):
        hth[side_of] = hth[side_of] * jnp.where(cond, 1.0, 0.0)

    sub = lax.broadcasted_iota(jnp.int32, (8, 128), 0)
    low_r, high_r = sub == 0, sub == 7

    def hydro_slab(p):
        q = lax.rem(p + 128 - whole, 64)
        before, after = lax.rem(q + 63, 64), lax.rem(q + 1, 64)
        big, j = q // 8, lax.rem(q, 8)
        back_by = lax.rem(128 - j, 128)
        c = [t1[q, f] for f in range(4)]
        thm, thp, phm, php, rm, rp = [], [], [], [], [], []
        for f in range(4):
            thm.append(jnp.where(low_th, pltpu.roll(hth[0, big, f], back_by, 1), pltpu.roll(c[f], 1, 1)))
            thp.append(jnp.where(high_th, pltpu.roll(hth[1, big, f], 7 - j, 1), pltpu.roll(c[f], 127, 1)))
            phm.append(jnp.where(first, pltpu.roll(t1[before, f], 8, 1), pltpu.roll(c[f], 8, 1)))
            php.append(jnp.where(last, pltpu.roll(t1[after, f], 120, 1), pltpu.roll(c[f], 120, 1)))
            lo = jnp.broadcast_to(hr2[0, q, pl.ds(f, 1), :], (8, 128))
            hi = jnp.broadcast_to(hr2[1, q, pl.ds(f, 1), :], (8, 128))
            rm.append(jnp.where(low_r, lo, pltpu.roll(c[f], 1, 0)))
            rp.append(jnp.where(high_r, hi, pltpu.roll(c[f], 7, 0)))
        new = updated(c, ((2, phm), (3, thm), (1, rm)), ((2, php), (3, thp), (1, rp)))
        return turn(new)

    def rho_message(p):
        return remote(fin.at[p, 0], rho_back.at[phi], rs, rr, {"phi": p})

    def vel_message(p):
        return remote(fin.at[p, pl.ds(1, 3)], back.at[phi], vs, vr, {"phi": p})

    own_rho = pltpu.make_async_copy(fin.at[phi, 0], rho_back.at[phi], ls.at[1])
    own_vel = pltpu.make_async_copy(fin.at[phi, pl.ds(1, 3)], back.at[phi], ls.at[2])

    def send(zoff, message, own_message):
        def one_slab(i, c):
            p = lax.rem(z + zoff, 8) * 8 + i

            @pl.when(p != phi)
            def _():
                message(p).start()

            @pl.when(p == phi)
            def _():
                own_message.start()

            return c

        lax.fori_loop(0, 8, one_slab, 0)

    def block(i, carry):
        start = lax.rem(z + spread(i), 8) * 8

        def slab(k, prev):
            cur = hydro_slab(start + k)
            out = blend(cur, prev)
            for f in range(4):
                fin[start + k, f] = out[f]
            return cur

        lax.fori_loop(0, 8, slab, hydro_slab(start - 1), unroll=UNROLL)

        @pl.when(i > 0)
        def _():
            send(spread(i - 1), rho_message, own_rho)

        @pl.when(i == 5)
        def _():
            send(4, vel_message, own_vel)

        return carry

    lax.fori_loop(0, 8, block, 0)
    send(0, rho_message, own_rho)
    for off in (1, 7, 0):
        send(off, vel_message, own_vel)

    wait_all(rho_back.at[pl.ds(0, 63)], (rs, rr))
    own_rho.wait()
    for g in range(4):
        t = jnp.concatenate([rho_back[where_of(j, g)] for j in range(16)], axis=0).T.reshape(16, 8, 128)
        for i in range(16):
            flat[pl.ds(i * 32 + 8 * g, 8), :] = t[i]
    k = row * 128 + lax.broadcasted_iota(jnp.int32, (16, 128), 1)
    radius = R_INNER + (k.astype(F32) + 0.5) * (1.0 - R_INNER) / NR
    seen = jnp.ones((16, 128), F32)
    total = jnp.zeros((16, 128), F32)
    for j in range(NTH):
        tilt = float(np.float32(1.0 + 0.5 * np.cos(np.pi * (j + 0.5) / NTH)))
        t = jnp.exp(flat[pl.ds(j, 16, stride=32), :] * (-KAPPA / NTH))
        total = total + tilt * ((1.0 - t) * seen)
        seen = seen * t
    light[...] = (1.0 / jnp.sqrt(radius)) * total

    own_light = pltpu.make_async_copy(light, table.at[row, xy, zl], ls.at[3])
    own_light.start()

    def up(n):
        to = {"phi": (half * 4 + lax.rem(zl + n, 4)) * 8 + xy}
        return remote(light, table.at[row, xy, zl], us.at[n], ur.at[n], to)

    def over(n, end):
        to = {"phi": ((1 - half) * 4 + lax.rem(zl + n, 4)) * 8 + xy}
        return remote(light, table.at[row, 8, end], us.at[4 + n], ur.at[4 + n], to)

    ends = ((1, 0, 0), (0, 7, 3))
    for n in (2, 1, 3):
        up(n).start()
    for end, at, plane in ends:

        @pl.when((xy == at) & (zl == plane))
        def _(end=end):
            for n in range(4):
                over(n, end).start()

    for off in (3, 5, 2, 6):
        send(off, vel_message, own_vel)
    for n in (1, 2, 3):
        up(n).wait()
    own_light.wait()
    for end, at, plane in ends:

        @pl.when((xy == at) & (zl == plane))
        def _(end=end):
            for n in range(4):
                over(n, end).wait_send()

        for pos in range(4):

            @pl.when((xy == at) & (zl == pos))
            def _(end=end, pos=pos, plane=plane):
                over((pos - plane) % 4, end).wait_recv()

    def part(q, pos, ssem, rsem, to):
        return remote(table.at[q, pos], table.at[q, pos], ssem, rsem, to)

    def outer(q, end, ssem, rsem, to):
        return remote(table.at[q, 8, end], table.at[q, 8, end], ssem, rsem, to)

    def to_chip(n, c):
        part(row, xy, ps.at[n], pr.at[n], chip(n)).start()
        for end, at, _ in ends:

            @pl.when(xy == at)
            def _(end=end):
                outer(row, end, hs.at[n], hrr.at[n], chip(n)).start()

        return c

    def give(q, pos, n):
        part(q, pos, gs.at[n], gr.at[n], sibling).start()
        for end, at, _ in ends:

            @pl.when(pos == at)
            def _(end=end):
                outer(q, end, hs.at[16 + n], hrr.at[16 + n], sibling).start()

    def source(n):
        m = lax.rem(xy * 2 + yh + 16 - n, 16)
        return m // 2, lax.rem(m, 2)

    def from_chip(n, c):
        pos, high = source(n)
        q = high * 2 + core
        part(q, pos, ps.at[n], pr.at[n], chip(n)).wait_recv()
        for end, at, _ in ends:

            @pl.when(pos == at)
            def _(end=end):
                outer(q, end, hs.at[n], hrr.at[n], chip(n)).wait_recv()

        give(q, pos, n)
        return c

    def finish(n, c):
        pos, high = source(n)
        q, other = high * 2 + core, high * 2 + 1 - core
        part(q, pos, gs.at[n], gr.at[n], sibling).wait_send()
        part(other, pos, gs.at[n], gr.at[n], sibling).wait_recv()
        for end, at, _ in ends:

            @pl.when(pos == at)
            def _(end=end):
                outer(q, end, hs.at[16 + n], hrr.at[16 + n], sibling).wait_send()
                outer(other, end, hs.at[16 + n], hrr.at[16 + n], sibling).wait_recv()

        return c

    def sent(n, c):
        part(row, xy, ps.at[n], pr.at[n], chip(n)).wait_send()
        for end, at, _ in ends:

            @pl.when(xy == at)
            def _(end=end):
                outer(row, end, hs.at[n], hrr.at[n], chip(n)).wait_send()

        return c

    lax.fori_loop(1, 16, to_chip, 0)
    give(row, xy, 0)
    lax.fori_loop(1, 16, from_chip, 0)
    lax.fori_loop(0, 16, finish, 0)
    lax.fori_loop(1, 16, sent, 0)
    wait_all(back.at[pl.ds(0, 63)], (vs, vr))
    own_vel.wait()


@functools.lru_cache(maxsize=None)
def sample_plan(rows_dev):
    yy = ((np.arange(NPIX) + 0.5) / NPIX * 2.0 - 1.0)[:, None]
    xx = ((np.arange(NPIX) + 0.5) / NPIX * 2.0 - 1.0)[None, :]
    u = (np.sqrt(xx * xx + yy * yy) - R_INNER) / (1.0 - R_INNER) * NR - 0.5
    v = (np.arctan2(yy, xx) + np.pi) / (2.0 * np.pi) * NPHI - 0.5
    blocks = NPIX // rows_dev
    plans = []
    for b in range(blocks):
        plan = []
        for c in range(NPIX // 128):
            cut = np.s_[b * rows_dev : (b + 1) * rows_dev, c * 128 : (c + 1) * 128]
            uu, vv = u[cut], v[cut]
            for q in range(NR // 128):
                hit = (uu > q * 128 - 1.01) & (uu < q * 128 + 128.01)
                if hit.any():
                    lo = int(np.floor((vv[hit].min() - 0.01) / 8))
                    hi = int(np.floor((np.floor(vv[hit].max() + 0.01) + 1) / 8))
                    plan.append((c, q, lo, hi - lo + 1))
        plans.append(plan)
    most = max(len(p) for p in plans)
    table = np.zeros((blocks, most, 4), np.int32)
    for b, plan in enumerate(plans):
        table[b, : len(plan)] = plan
    return table


def last_kernel(plan_ref, u_ref, v_ref, rho_src, vel_src, w_ref, rho_ref, vel_ref, out_ref, acc, *, most):
    phi, row = lax.axis_index("phi"), lax.axis_index("row")
    for f in range(4):
        for g in range(4):
            x = jnp.concatenate(
                [rho_src[where_of(j, g)] if f == 0 else vel_src[where_of(j, g), f - 1] for j in range(16)], axis=0
            )
            t = x.T.reshape(16, 8, 128)
            if f == 0:
                rho_ref[:, 8 * g : 8 * g + 8, :] = t
            else:
                vel_ref[f - 1, :, 8 * g : 8 * g + 8, :] = t
    spot = phi * 4 + row
    first_tile = phi // 32 * 64
    acc[...] = jnp.zeros_like(acc)
    sub = lax.broadcasted_iota(jnp.int32, (8, 128), 0)

    def task(t, carry):
        word = plan_ref[spot * most + t]
        chunk, q = word % 8, word // 8 % 4
        lo, count = word // 32 % 256 - 1, word // 8192
        cols = pl.ds(pl.multiple_of(chunk * 128, 128), 128)
        u, v = u_ref[:, cols], v_ref[:, cols]
        floor = jnp.floor(u)
        part = u - floor
        k = floor.astype(jnp.int32) - q * 128 + jnp.where(sub >= 4, 1, 0)
        weight = jnp.where(sub >= 4, part, 1.0 - part)
        weight = jnp.where((k >= 0) & (k < 128), weight, 0.0)
        k = jnp.clip(k, 0, 127)

        def tiles(i, total):
            base = (lo + i) * 8
            near = lo + i - first_tile
            slab = jnp.where(near < 0, 32, jnp.where(near > 63, 33, near // 2 % 8 * 4 + near // 16))
            start = pl.multiple_of(slab * 16 + (near + 2) % 2 * 8, 8)
            block = w_ref[q, pl.ds(start, 8), :]
            shifted = v - base.astype(F32)
            for s in range(8):
                line = jnp.broadcast_to(block[s : s + 1, :], (8, 128))
                got = jnp.take_along_axis(line, k, axis=1, mode="promise_in_bounds")
                total = total + jnp.maximum(1.0 - jnp.abs(shifted - float(s)), 0.0) * got
            return total

        total = lax.fori_loop(0, count, tiles, jnp.zeros((8, 128), F32))
        acc[:, cols] = acc[:, cols] + weight * total
        return carry

    lax.fori_loop(0, most, task, 0)
    out_ref[...] = acc[0:4, :] + acc[4:8, :]


def body(density, velocity, shifts, fractions):
    sds = lambda *s: jax.ShapeDtypeStruct(s, F32)
    dma = lambda *s: pltpu.SemaphoreType.DMA(s)
    vmem = lambda *s: pltpu.VMEM(s, F32)
    one = pltpu.SemaphoreType.DMA
    back, table, rho_back, upos, vpos = pl.pallas_call(
        main_kernel, name="main", out_shape=(sds(64, 3, 8, 128), sds(4, 9, 4, 16, 128), sds(64, 8, 128), sds(8, 1024), sds(8, 1024)),
        in_specs=[SM, SM, VM, VM], out_specs=(ANY, ANY, VM, VM, VM),
        scratch_shapes=[
            vmem(4, 4, 144, 128), vmem(2, 16, 128), vmem(2, 4, 32, 128), vmem(2, 16, 128), vmem(2, 128, 128),
            vmem(64, 4, 8, 128), vmem(64, 4, 8, 128), vmem(64, 4, 8, 128),
            vmem(2, 8, 4, 8, 128), vmem(2, 64, 4, 128), vmem(2, 8, 4, 8, 128), vmem(2, 64, 4, 128),
            vmem(64, 4, 8, 128), vmem(512, 128), vmem(16, 128),
            dma(6), dma(6), one, one, dma(4), dma(4), one, one, one, one, dma(4), dma(8), dma(8),
            dma(32), dma(32), dma(16), dma(16), dma(16), dma(16),
        ],
        compiler_params=pltpu.CompilerParams(collective_id=0, has_side_effects=True),
    )(shifts, fractions, density, velocity)
    plan = sample_plan(4)
    most = plan.shape[1]
    words = plan[..., 0] + 8 * plan[..., 1] + 32 * (plan[..., 2] + 1) + 8192 * plan[..., 3]
    return pl.pallas_call(
        functools.partial(last_kernel, most=most), name="last",
        out_shape=(sds(16, 32, 128), sds(3, 16, 32, 128), sds(4, 1024)),
        in_specs=[SM, VM, VM, VM, VM, VM], out_specs=(VM, VM, VM),
        scratch_shapes=[pltpu.VMEM((8, 1024), F32)],
    )(jnp.asarray(words.reshape(-1)), upos, vpos, rho_back, back, table.reshape(4, 576, 128))


def solution(mesh):
    in_specs = (P("phi", None, "row"), P(None, "phi", None, "row"), P("row"), P("row"))
    out_specs = (P("phi", None, "row"), P(None, "phi", None, "row"), P(("phi", "row"), None))
    return jax.shard_map(body, mesh=mesh, in_specs=in_specs, out_specs=out_specs, check_vma=False)
```

```python
import functools

import jax
import jax.numpy as jnp
import numpy as np
from jax import lax
from jax.experimental import pallas as pl
from jax.experimental.pallas import tpu as pltpu
from jax.sharding import PartitionSpec as P

MESH = pl.DeviceIdType.MESH
BAND = 8
NPIX = 1024
NPHI = 1024
NR = 512
NTH = 32
UNROLL = 4
KAPPA = 1.5
R_INNER = 0.2
F32 = jnp.float32
VM = pl.BlockSpec(memory_space=pltpu.VMEM)
SM = pl.BlockSpec(memory_space=pltpu.SMEM)
ANY = pl.BlockSpec(memory_space=pl.ANY)


def where_of(band, group):
    return (band % 8) * 8 + group * 2 + band // 8


def lanes():
    return lax.broadcasted_iota(jnp.int32, (8, 128), 1)


def rolled(tiles, by, axis=1):
    return [pltpu.roll(t, by, axis) for t in tiles]


def conserved(q):
    return [q[0], q[0] * q[1], q[0] * q[2], q[0] * q[3]]


def side(q, comp, offset):
    m = q[0] * (0.5 * q[comp] + offset)
    out = [m, m * q[1], m * q[2], m * q[3]]
    out[comp] = out[comp] + 0.5 * q[0]
    return out


def updated(here, lower, upper):
    total = None
    for (comp, low), (_, high) in zip(lower, upper):
        p, m = side(low, comp, 0.75), side(high, comp, -0.75)
        part = [b - a for a, b in zip(p, m)]
        total = part if total is None else [s + t for s, t in zip(total, part)]
    new = [0.775 * c - 0.05 * t for c, t in zip(conserved(here), total)]
    inv = 1.0 / new[0]
    return [new[0], new[1] * inv, new[2] * inv, new[3] * inv]


def spread(i):
    return jnp.where(i % 2 == 0, 4 + i // 2, 4 - (i + 1) // 2)


def signal(peer):
    pl.semaphore_signal(pltpu.get_barrier_semaphore(), inc=1, device_id=peer, device_id_type=MESH)


def remote(src, dst, ssem, rsem, to):
    return pltpu.make_async_remote_copy(src, dst, ssem, rsem, device_id=to, device_id_type=MESH)


def wait_all(ref, sems):
    for sem in sems:
        pltpu.make_async_copy(ref, ref, sem).wait()


def main_kernel(
    shift_ref, frac_ref, rho_in, vel_in, back, table, rho_back, u_ref, v_ref,
    rho_ref, vel_ref, pad, edge, hphi, hr, ht, stepped, cyc, t1, th_edge, r_edge, hth, hr2, fin, flat, light,
    es, er, as_, ar, bs, br, rs, rr, vs, vr, ls, us, ur, hs, hrr, ps, pr, gs, gr,
):
    phi, row = lax.axis_index("phi"), lax.axis_index("row")
    z, x, y = phi // 8, lax.rem(phi // 2, 4), lax.rem(phi, 2)
    half, zl, xy = z // 4, lax.rem(z, 4), lax.rem(phi, 8)
    core, yh = lax.rem(row, 2), row // 2
    band = row * 16 + y * 8 + z

    def at_band(b):
        j = lax.rem(b, 16)
        return {"phi": lax.rem(j, 8) * 8 + x * 2 + j // 8, "row": b // 16}

    def at_group(g):
        return {"phi": z * 8 + g * 2 + y}

    def chip(n):
        m = lax.rem(xy * 2 + yh + n, 16)
        return {"phi": z * 8 + m // 2, "row": lax.rem(m, 2) * 2 + core}

    sibling = {"row": yh * 2 + 1 - core}
    phi_low, phi_high = {"phi": lax.rem(phi + 63, 64)}, {"phi": lax.rem(phi + 1, 64)}
    row_low, row_high = {"row": lax.rem(row + 3, 4)}, {"row": lax.rem(row + 1, 4)}
    band_low, band_high = at_band(lax.rem(band + 63, 64)), at_band(lax.rem(band + 1, 64))
    group_low, group_high = at_group(lax.rem(x + 3, 4)), at_group(lax.rem(x + 1, 4))

    loads = [
        pltpu.make_async_copy(rho_in, rho_ref, ls.at[4]),
        pltpu.make_async_copy(vel_in, vel_ref, ls.at[5]),
    ]
    for c in loads:
        c.start()

    def greet_phi(i, c):
        peer = lax.rem(z + spread(i // 8), 8) * 8 + lax.rem(i, 8)

        @pl.when(peer != phi)
        def _():
            signal({"phi": peer})

        return c

    def greet_chip(n, c):
        signal(chip(n))
        return c

    lax.fori_loop(0, 64, greet_phi, 0)
    for peer in (row_low, row_high, band_low, band_high, sibling):
        signal(peer)
    lax.fori_loop(1, 16, greet_chip, 0)

    for c in loads:
        c.wait()
    for f in range(4):
        for g in range(4):
            src = rho_ref[:, 8 * g : 8 * g + 8, :] if f == 0 else vel_ref[f - 1, :, 8 * g : 8 * g + 8, :]
            t = src.reshape(128, 128).T
            pad[f, g, 8:136, :] = t
            edge[0, pl.ds(f * 4 + g, 1), :] = t[0:1, :]
            edge[1, pl.ds(f * 4 + g, 1), :] = t[127:128, :]
    pl.semaphore_wait(pltpu.get_barrier_semaphore(), 83)
    copies = [
        remote(rho_ref.at[15], hphi.at[0, 0], es.at[0], er.at[0], phi_high),
        remote(vel_ref.at[:, 15], hphi.at[0, pl.ds(1, 3)], es.at[1], er.at[1], phi_high),
        remote(rho_ref.at[0], hphi.at[1, 0], es.at[2], er.at[2], phi_low),
        remote(vel_ref.at[:, 0], hphi.at[1, pl.ds(1, 3)], es.at[3], er.at[3], phi_low),
        remote(edge.at[1], hr.at[0], es.at[4], er.at[4], row_high),
        remote(edge.at[0], hr.at[1], es.at[5], er.at[5], row_low),
    ]
    for c in copies:
        c.start()
    for c in copies:
        c.wait()
    has_low = jnp.where(row > 0, 1.0, 0.0)
    has_high = jnp.where(row < 3, 1.0, 0.0)
    for pair in range(2):
        ht[pair] = jnp.concatenate([hphi[s, 2 * pair + f] for f in range(2) for s in range(2)], axis=0).T
    for f in range(4):
        for g in range(4):
            pad[f, g, 7:8, :] = hr[0, pl.ds(f * 4 + g, 1), :] * has_low
            pad[f, g, 136:137, :] = hr[1, pl.ds(f * 4 + g, 1), :] * has_high

    lane = lanes()
    lane8 = lane % 8
    first, last = lane < 8, lane >= 120
    low_th, high_th = lane8 == 0, lane8 == 7
    zero = jnp.zeros((8, 128), F32)

    def band_at(i):
        return lax.rem(z + spread(i // 2), 8) + 8 * (i % 2)

    def spot(i, g):
        j = band_at(i)
        return lax.rem(j, 8) * 8 + g * 2 + j // 8

    own = pltpu.make_async_copy(stepped.at[phi], cyc.at[phi], ls.at[0])

    def send_tiles(i):
        for g in range(4):
            d = spot(i, g)

            @pl.when(d != phi)
            def _():
                remote(stepped.at[d], cyc.at[phi], as_, ar, {"phi": d}).start()

            @pl.when(d == phi)
            def _():
                own.start()

    def step(i, carry):
        base = pl.multiple_of(8 * band_at(i), 8)
        here = [[pad[f, g, pl.ds(base + 8, 8), :] for f in range(4)] for g in range(4)]
        side_edge = [ht[pair, pl.ds(base, 8), :] for pair in range(2)]
        for g in range(4):
            c = here[g]
            before = [pad[f, g, pl.ds(base, 16), :][7:15] for f in range(4)]
            after = [pad[f, g, pl.ds(base + 8, 16), :][1:9] for f in range(4)]
            below = [pltpu.roll(here[g - 1][f], 121, 1) if g > 0 else zero for f in range(4)]
            above = [pltpu.roll(here[g + 1][f], 7, 1) if g < 3 else zero for f in range(4)]
            thm = [jnp.where(low_th, lo, t) for lo, t in zip(below, rolled(c, 1))]
            thp = [jnp.where(high_th, hi, t) for hi, t in zip(above, rolled(c, 127))]
            offs = [(f % 2) * 64 + g * 8 for f in range(4)]
            below = [pltpu.roll(side_edge[f // 2], (128 - offs[f]) % 128, 1) for f in range(4)]
            above = [pltpu.roll(side_edge[f // 2], (120 - offs[f] - 32) % 128, 1) for f in range(4)]
            phm = [jnp.where(first, lo, t) for lo, t in zip(below, rolled(c, 8))]
            php = [jnp.where(last, hi, t) for hi, t in zip(above, rolled(c, 120))]
            new = updated(c, ((2, phm), (3, thm), (1, before)), ((2, php), (3, thp), (1, after)))
            d = spot(i, g)
            for f in range(4):
                stepped[d, f] = new[f]

        @pl.when(i > 0)
        def _():
            send_tiles(i - 1)

        return carry

    lax.fori_loop(0, 16, step, 0)
    send_tiles(15)

    local = z + 8 * y
    shift = shift_ref[local]
    w = frac_ref[local]
    whole, remain = shift // 16, shift % 16
    one, two = 8 * remain, 8 * (remain + 1)
    two_roll = lax.rem(two, 128)
    keep_one, keep_two = lane >= one, lane >= two

    def turn(tiles):
        return rolled(tiles, one) + rolled(tiles, two_roll)

    def blend(cur, prev):
        out = []
        for f in range(4):
            lead = jnp.where(keep_one, cur[f], prev[f])
            trail = jnp.where(keep_two, cur[4 + f], prev[4 + f])
            out.append((1.0 - w) * lead + w * trail)
        return out

    def cycle_slab(p):
        slab = lax.rem(p + 128 - whole, 64)
        return turn([cyc[slab, f] for f in range(4)])

    def move(big, prev):
        top, bottom = [None] * 4, [None] * 4
        for j in range(8):
            cur = cycle_slab(big * 8 + j)
            out = blend(cur, prev)
            prev = cur
            hi, lo = rolled(out, (j - 7) % 128), rolled(out, j) if j else out
            for f in range(4):
                t = out[f]
                t1[big * 8 + j, f] = t
                top[f] = hi[f] if j == 0 else jnp.where(lane8 == j, hi[f], top[f])
                bottom[f] = lo[f] if j == 0 else jnp.where(lane8 == j, lo[f], bottom[f])
                r_edge[0, big * 8 + j, pl.ds(f, 1), :] = t[0:1, :]
                r_edge[1, big * 8 + j, pl.ds(f, 1), :] = t[7:8, :]
        for f in range(4):
            th_edge[0, big, f] = bottom[f]
            th_edge[1, big, f] = top[f]
        return prev

    pixel = (phi * 4 + row) * 4 + lax.broadcasted_iota(jnp.int32, (8, 1024), 0) % 4
    column = lax.broadcasted_iota(jnp.int32, (8, 1024), 1)
    yy = (pixel.astype(F32) + 0.5) / NPIX * 2.0 - 1.0
    xx = (column.astype(F32) + 0.5) / NPIX * 2.0 - 1.0
    dist = jnp.sqrt(xx * xx + yy * yy)
    u_ref[...] = (dist - R_INNER) / (1.0 - R_INNER) * NR - 0.5
    v_ref[...] = (jnp.arctan2(yy, xx) + jnp.pi) / (2.0 * jnp.pi) * NPHI - 0.5

    wait_all(cyc.at[pl.ds(0, 63)], (as_, ar))
    own.wait()
    lax.fori_loop(0, 8, move, cycle_slab(-1))
    copies = [
        remote(r_edge.at[1], hr2.at[0], bs.at[0], br.at[0], band_high),
        remote(r_edge.at[0], hr2.at[1], bs.at[1], br.at[1], band_low),
        remote(th_edge.at[1], hth.at[0], bs.at[2], br.at[2], group_high),
        remote(th_edge.at[0], hth.at[1], bs.at[3], br.at[3], group_low),
    ]
    for c in copies:
        c.start()
    for c in copies:
        c.wait()
    for side_of, cond in enumerate((band > 0, band < 63)):
        hr2[side_of] = hr2[side_of] * jnp.where(cond, 1.0, 0.0)
    for side_of, cond in enumerate((x > 0, x < 3)):
        hth[side_of] = hth[side_of] * jnp.where(cond, 1.0, 0.0)

    sub = lax.broadcasted_iota(jnp.int32, (8, 128), 0)
    low_r, high_r = sub == 0, sub == 7

    def at_slab(p):
        return lax.rem(p + 192 - whole, 64)

    def enter(p):
        here = [t1[at_slab(p), f] for f in range(4)]
        behind = rolled([t1[at_slab(p - 1), f] for f in range(4)], 8)
        return here, behind, rolled(here, 120)

    def hydro_slab(p, window):
        c, phm_far, c_up = window
        q = at_slab(p)
        big, j = q // 8, lax.rem(q, 8)
        ahead = [t1[at_slab(p + 1), f] for f in range(4)]
        ahead_up, c_on = rolled(ahead, 120), rolled(c, 8)
        phm = [jnp.where(first, a, b) for a, b in zip(phm_far, c_on)]
        php = [jnp.where(last, a, b) for a, b in zip(ahead_up, c_up)]
        below = rolled([hth[0, big, f] for f in range(4)], lax.rem(128 - j, 128))
        above = rolled([hth[1, big, f] for f in range(4)], 7 - j)
        thm = [jnp.where(low_th, a, b) for a, b in zip(below, rolled(c, 1))]
        thp = [jnp.where(high_th, a, b) for a, b in zip(above, rolled(c, 127))]
        below = [jnp.broadcast_to(hr2[0, q, pl.ds(f, 1), :], (8, 128)) for f in range(4)]
        above = [jnp.broadcast_to(hr2[1, q, pl.ds(f, 1), :], (8, 128)) for f in range(4)]
        rm = [jnp.where(low_r, a, b) for a, b in zip(below, rolled(c, 1, 0))]
        rp = [jnp.where(high_r, a, b) for a, b in zip(above, rolled(c, 7, 0))]
        new = updated(c, ((2, phm), (3, thm), (1, rm)), ((2, php), (3, thp), (1, rp)))
        return turn(new), (ahead, c_on, ahead_up)

    def rho_message(p):
        return remote(fin.at[p, 0], rho_back.at[phi], rs, rr, {"phi": p})

    def vel_message(p):
        return remote(fin.at[p, pl.ds(1, 3)], back.at[phi], vs, vr, {"phi": p})

    own_rho = pltpu.make_async_copy(fin.at[phi, 0], rho_back.at[phi], ls.at[1])
    own_vel = pltpu.make_async_copy(fin.at[phi, pl.ds(1, 3)], back.at[phi], ls.at[2])

    def send_far(zoff, message):
        def one_slab(i, c):
            message(lax.rem(z + zoff, 8) * 8 + i).start()
            return c

        lax.fori_loop(0, 8, one_slab, 0, unroll=2)

    def send(zoff, message, own_message):
        def one_slab(i, c):
            p = lax.rem(z + zoff, 8) * 8 + i

            @pl.when(p != phi)
            def _():
                message(p).start()

            @pl.when(p == phi)
            def _():
                own_message.start()

            return c

        lax.fori_loop(0, 8, one_slab, 0)

    def block(i, carry):
        start = lax.rem(z + spread(i), 8) * 8

        def slab(k, carry):
            prev, window = carry
            cur, window = hydro_slab(start + k, window)
            out = blend(cur, prev)
            for f in range(4):
                fin[start + k, f] = out[f]
            return cur, window

        lax.fori_loop(0, 8, slab, hydro_slab(start - 1, enter(start - 1)), unroll=UNROLL)

        @pl.when(i > 0)
        def _():
            send_far(spread(i - 1), rho_message)

        @pl.when(i == 5)
        def _():
            send_far(4, vel_message)

        return carry

    lax.fori_loop(0, 8, block, 0)
    send(0, rho_message, own_rho)
    send_far(1, vel_message)
    send_far(7, vel_message)
    send(0, vel_message, own_vel)

    wait_all(rho_back.at[pl.ds(0, 63)], (rs, rr))
    own_rho.wait()
    for g in range(4):
        t = jnp.concatenate([rho_back[where_of(j, g)] for j in range(16)], axis=0).T.reshape(16, 8, 128)
        for i in range(16):
            flat[pl.ds(i * 32 + 8 * g, 8), :] = t[i]
    k = row * 128 + lax.broadcasted_iota(jnp.int32, (16, 128), 1)
    radius = R_INNER + (k.astype(F32) + 0.5) * (1.0 - R_INNER) / NR
    seen = jnp.ones((16, 128), F32)
    total = jnp.zeros((16, 128), F32)
    for j in range(NTH):
        tilt = float(np.float32(1.0 + 0.5 * np.cos(np.pi * (j + 0.5) / NTH)))
        t = jnp.exp(flat[pl.ds(j, 16, stride=32), :] * (-KAPPA / NTH))
        total = total + tilt * ((1.0 - t) * seen)
        seen = seen * t
    light[...] = (1.0 / jnp.sqrt(radius)) * total

    own_light = pltpu.make_async_copy(light, table.at[row, xy, zl], ls.at[3])
    own_light.start()

    def up(n):
        to = {"phi": (half * 4 + lax.rem(zl + n, 4)) * 8 + xy}
        return remote(light, table.at[row, xy, zl], us.at[n], ur.at[n], to)

    def over(n, end):
        to = {"phi": ((1 - half) * 4 + lax.rem(zl + n, 4)) * 8 + xy}
        return remote(light, table.at[row, 8, end], us.at[4 + n], ur.at[4 + n], to)

    ends = ((1, 0, 0), (0, 7, 3))
    for n in (2, 1, 3):
        up(n).start()
    for end, at, plane in ends:

        @pl.when((xy == at) & (zl == plane))
        def _(end=end):
            for n in range(4):
                over(n, end).start()

    for off in (3, 5, 2, 6):
        send_far(off, vel_message)
    for n in (1, 2, 3):
        up(n).wait()
    own_light.wait()
    for end, at, plane in ends:

        @pl.when((xy == at) & (zl == plane))
        def _(end=end):
            for n in range(4):
                over(n, end).wait_send()

        for pos in range(4):

            @pl.when((xy == at) & (zl == pos))
            def _(end=end, pos=pos, plane=plane):
                over((pos - plane) % 4, end).wait_recv()

    def part(q, pos, ssem, rsem, to):
        return remote(table.at[q, pos], table.at[q, pos], ssem, rsem, to)

    def outer(q, end, ssem, rsem, to):
        return remote(table.at[q, 8, end], table.at[q, 8, end], ssem, rsem, to)

    def to_chip(n, c):
        part(row, xy, ps.at[n], pr.at[n], chip(n)).start()
        for end, at, _ in ends:

            @pl.when(xy == at)
            def _(end=end):
                outer(row, end, hs.at[n], hrr.at[n], chip(n)).start()

        return c

    def give(q, pos, n):
        part(q, pos, gs.at[n], gr.at[n], sibling).start()
        for end, at, _ in ends:

            @pl.when(pos == at)
            def _(end=end):
                outer(q, end, hs.at[16 + n], hrr.at[16 + n], sibling).start()

    def source(n):
        m = lax.rem(xy * 2 + yh + 16 - n, 16)
        return m // 2, lax.rem(m, 2)

    def from_chip(n, c):
        pos, high = source(n)
        q = high * 2 + core
        part(q, pos, ps.at[n], pr.at[n], chip(n)).wait_recv()
        for end, at, _ in ends:

            @pl.when(pos == at)
            def _(end=end):
                outer(q, end, hs.at[n], hrr.at[n], chip(n)).wait_recv()

        give(q, pos, n)
        return c

    def finish(n, c):
        pos, high = source(n)
        q, other = high * 2 + core, high * 2 + 1 - core
        part(q, pos, gs.at[n], gr.at[n], sibling).wait_send()
        part(other, pos, gs.at[n], gr.at[n], sibling).wait_recv()
        for end, at, _ in ends:

            @pl.when(pos == at)
            def _(end=end):
                outer(q, end, hs.at[16 + n], hrr.at[16 + n], sibling).wait_send()
                outer(other, end, hs.at[16 + n], hrr.at[16 + n], sibling).wait_recv()

        return c

    def sent(n, c):
        part(row, xy, ps.at[n], pr.at[n], chip(n)).wait_send()
        for end, at, _ in ends:

            @pl.when(xy == at)
            def _(end=end):
                outer(row, end, hs.at[n], hrr.at[n], chip(n)).wait_send()

        return c

    lax.fori_loop(1, 16, to_chip, 0)
    give(row, xy, 0)
    lax.fori_loop(1, 16, from_chip, 0)
    lax.fori_loop(0, 16, finish, 0)
    lax.fori_loop(1, 16, sent, 0)
    wait_all(back.at[pl.ds(0, 63)], (vs, vr))
    own_vel.wait()


@functools.lru_cache(maxsize=None)
def sample_plan(rows_dev):
    yy = ((np.arange(NPIX) + 0.5) / NPIX * 2.0 - 1.0)[:, None]
    xx = ((np.arange(NPIX) + 0.5) / NPIX * 2.0 - 1.0)[None, :]
    u = (np.sqrt(xx * xx + yy * yy) - R_INNER) / (1.0 - R_INNER) * NR - 0.5
    v = (np.arctan2(yy, xx) + np.pi) / (2.0 * np.pi) * NPHI - 0.5
    blocks = NPIX // rows_dev
    plans = []
    for b in range(blocks):
        plan = []
        for c in range(NPIX // 128):
            cut = np.s_[b * rows_dev : (b + 1) * rows_dev, c * 128 : (c + 1) * 128]
            uu, vv = u[cut], v[cut]
            for q in range(NR // 128):
                hit = (uu > q * 128 - 1.01) & (uu < q * 128 + 128.01)
                if hit.any():
                    lo = int(np.floor((vv[hit].min() - 0.01) / 8))
                    hi = int(np.floor((np.floor(vv[hit].max() + 0.01) + 1) / 8))
                    plan.append((c, q, lo, hi - lo + 1))
        plans.append(plan)
    most = max(len(p) for p in plans)
    table = np.zeros((blocks, most, 4), np.int32)
    for b, plan in enumerate(plans):
        table[b, : len(plan)] = plan
    return table


def last_kernel(plan_ref, u_ref, v_ref, rho_src, vel_src, w_ref, rho_ref, vel_ref, out_ref, acc, *, most):
    phi, row = lax.axis_index("phi"), lax.axis_index("row")
    for f in range(4):
        for g in range(4):
            x = jnp.concatenate(
                [rho_src[where_of(j, g)] if f == 0 else vel_src[where_of(j, g), f - 1] for j in range(16)], axis=0
            )
            t = x.T.reshape(16, 8, 128)
            if f == 0:
                rho_ref[:, 8 * g : 8 * g + 8, :] = t
            else:
                vel_ref[f - 1, :, 8 * g : 8 * g + 8, :] = t
    spot = phi * 4 + row
    first_tile = phi // 32 * 64
    acc[...] = jnp.zeros_like(acc)
    sub = lax.broadcasted_iota(jnp.int32, (8, 128), 0)

    def task(t, carry):
        word = plan_ref[spot * most + t]
        chunk, q = word % 8, word // 8 % 4
        lo, count = word // 32 % 256 - 1, word // 8192
        cols = pl.ds(pl.multiple_of(chunk * 128, 128), 128)
        u, v = u_ref[:, cols], v_ref[:, cols]
        floor = jnp.floor(u)
        part = u - floor
        k = floor.astype(jnp.int32) - q * 128 + jnp.where(sub >= 4, 1, 0)
        weight = jnp.where(sub >= 4, part, 1.0 - part)
        weight = jnp.where((k >= 0) & (k < 128), weight, 0.0)
        k = jnp.clip(k, 0, 127)

        def tile(near, total):
            shifted = v - ((near + first_tile) * 8).astype(F32)
            slab = jnp.where(near < 0, 32, jnp.where(near > 63, 33, near // 2 % 8 * 4 + near // 16))
            start = pl.multiple_of(slab * 16 + (near + 2) % 2 * 8, 8)
            block = w_ref[q, pl.ds(start, 8), :]
            for s in range(8):
                line = jnp.broadcast_to(block[s : s + 1, :], (8, 128))
                got = jnp.take_along_axis(line, k, axis=1, mode="promise_in_bounds")
                total = total + jnp.maximum(1.0 - jnp.abs(shifted - float(s)), 0.0) * got
            return total

        def pair(i, totals):
            near = lo - first_tile + 2 * i
            return tile(near, totals[0]), tile(near + 1, totals[1])

        nothing = jnp.zeros((8, 128), F32)
        even, odd = lax.fori_loop(0, (count + 1) // 2, pair, (nothing, nothing))
        total = even + odd
        acc[:, cols] = acc[:, cols] + weight * total
        return carry

    lax.fori_loop(0, most, task, 0)
    out_ref[...] = acc[0:4, :] + acc[4:8, :]


def body(density, velocity, shifts, fractions):
    sds = lambda *s: jax.ShapeDtypeStruct(s, F32)
    dma = lambda *s: pltpu.SemaphoreType.DMA(s)
    vmem = lambda *s: pltpu.VMEM(s, F32)
    one = pltpu.SemaphoreType.DMA
    back, table, rho_back, upos, vpos = pl.pallas_call(
        main_kernel, name="main", out_shape=(sds(64, 3, 8, 128), sds(4, 9, 4, 16, 128), sds(64, 8, 128), sds(8, 1024), sds(8, 1024)),
        in_specs=[SM, SM, ANY, ANY], out_specs=(ANY, ANY, VM, VM, VM),
        scratch_shapes=[
            vmem(16, 32, 128), vmem(3, 16, 32, 128), vmem(4, 4, 144, 128), vmem(2, 16, 128), vmem(2, 4, 32, 128), vmem(2, 16, 128), vmem(2, 128, 128),
            vmem(64, 4, 8, 128), vmem(64, 4, 8, 128), vmem(64, 4, 8, 128),
            vmem(2, 8, 4, 8, 128), vmem(2, 64, 4, 128), vmem(2, 8, 4, 8, 128), vmem(2, 64, 4, 128),
            vmem(64, 4, 8, 128), vmem(512, 128), vmem(16, 128),
            dma(6), dma(6), one, one, dma(4), dma(4), one, one, one, one, dma(6), dma(8), dma(8),
            dma(32), dma(32), dma(16), dma(16), dma(16), dma(16),
        ],
        compiler_params=pltpu.CompilerParams(collective_id=0, has_side_effects=True),
    )(shifts, fractions, density, velocity)
    plan = sample_plan(4)
    most = plan.shape[1]
    words = plan[..., 0] + 8 * plan[..., 1] + 32 * (plan[..., 2] + 1) + 8192 * plan[..., 3]
    return pl.pallas_call(
        functools.partial(last_kernel, most=most), name="last",
        out_shape=(sds(16, 32, 128), sds(3, 16, 32, 128), sds(4, 1024)),
        in_specs=[SM, VM, VM, VM, VM, VM], out_specs=(VM, VM, VM),
        scratch_shapes=[pltpu.VMEM((8, 1024), F32)],
    )(jnp.asarray(words.reshape(-1)), upos, vpos, rho_back, back, table.reshape(4, 576, 128))


def solution(mesh):
    in_specs = (P("phi", None, "row"), P(None, "phi", None, "row"), P("row"), P("row"))
    out_specs = (P("phi", None, "row"), P(None, "phi", None, "row"), P(("phi", "row"), None))
    return jax.shard_map(body, mesh=mesh, in_specs=in_specs, out_specs=out_specs, check_vma=False)
```

```python
import functools

import jax
import jax.numpy as jnp
import numpy as np
from jax import lax
from jax.experimental import pallas as pl
from jax.experimental.pallas import tpu as pltpu
from jax.sharding import PartitionSpec as P

MESH = pl.DeviceIdType.MESH
BAND = 8
NPIX = 1024
NPHI = 1024
NR = 512
NTH = 32
UNROLL = 4
KAPPA = 1.5
R_INNER = 0.2
F32 = jnp.float32
VM = pl.BlockSpec(memory_space=pltpu.VMEM)
SM = pl.BlockSpec(memory_space=pltpu.SMEM)
ANY = pl.BlockSpec(memory_space=pl.ANY)


def where_of(band, group):
    return (band % 8) * 8 + group * 2 + band // 8


def lanes():
    return lax.broadcasted_iota(jnp.int32, (8, 128), 1)


def rolled(tiles, by, axis=1):
    return [pltpu.roll(t, by, axis) for t in tiles]


def conserved(q):
    return [q[0], q[0] * q[1], q[0] * q[2], q[0] * q[3]]


def side(q, comp, offset):
    m = q[0] * (0.5 * q[comp] + offset)
    out = [m, m * q[1], m * q[2], m * q[3]]
    out[comp] = out[comp] + 0.5 * q[0]
    return out


def updated(here, lower, upper):
    total = None
    for (comp, low), (_, high) in zip(lower, upper):
        p, m = side(low, comp, 0.75), side(high, comp, -0.75)
        part = [b - a for a, b in zip(p, m)]
        total = part if total is None else [s + t for s, t in zip(total, part)]
    new = [0.775 * c - 0.05 * t for c, t in zip(conserved(here), total)]
    inv = 1.0 / new[0]
    return [new[0], new[1] * inv, new[2] * inv, new[3] * inv]


def spread(i):
    return jnp.where(i % 2 == 0, 4 + i // 2, 4 - (i + 1) // 2)


def signal(peer):
    pl.semaphore_signal(pltpu.get_barrier_semaphore(), inc=1, device_id=peer, device_id_type=MESH)


def remote(src, dst, ssem, rsem, to):
    return pltpu.make_async_remote_copy(src, dst, ssem, rsem, device_id=to, device_id_type=MESH)


def wait_all(ref, sems):
    for sem in sems:
        pltpu.make_async_copy(ref, ref, sem).wait()


def main_kernel(
    shift_ref, frac_ref, rho_in, vel_in, back, table, rho_back, u_ref, v_ref,
    rho_ref, vel_ref, pad, edge, hphi, hr, ht, stepped, cyc, t1, th_edge, r_edge, hth, hr2, fin, flat, light,
    word, es, er, as_, ar, bs, br, rs, rr, vs, vr, ls, us, ur, hs, hrr, ps, pr, gs, gr,
):
    phi, row = lax.axis_index("phi"), lax.axis_index("row")
    z, x, y = phi // 8, lax.rem(phi // 2, 4), lax.rem(phi, 2)
    half, zl, xy = z // 4, lax.rem(z, 4), lax.rem(phi, 8)
    core, yh = lax.rem(row, 2), row // 2
    band = row * 16 + y * 8 + z

    def at_band(b):
        j = lax.rem(b, 16)
        return {"phi": lax.rem(j, 8) * 8 + x * 2 + j // 8, "row": b // 16}

    def at_group(g):
        return {"phi": z * 8 + g * 2 + y}

    def chip(n):
        m = lax.rem(xy * 2 + yh + n, 16)
        return {"phi": z * 8 + m // 2, "row": lax.rem(m, 2) * 2 + core}

    sibling = {"row": yh * 2 + 1 - core}
    phi_low, phi_high = {"phi": lax.rem(phi + 63, 64)}, {"phi": lax.rem(phi + 1, 64)}
    row_low, row_high = {"row": lax.rem(row + 3, 4)}, {"row": lax.rem(row + 1, 4)}
    band_low, band_high = at_band(lax.rem(band + 63, 64)), at_band(lax.rem(band + 1, 64))
    group_low, group_high = at_group(lax.rem(x + 3, 4)), at_group(lax.rem(x + 1, 4))

    loads = [
        pltpu.make_async_copy(rho_in, rho_ref, ls.at[4]),
        pltpu.make_async_copy(vel_in, vel_ref, ls.at[5]),
    ]
    for c in loads:
        c.start()

    def plane(d):
        return {"phi": z * 8 + lax.rem(xy + d, 8)}

    def beyond(d):
        return {"phi": lax.rem(z + d, 8) * 8 + xy}

    def greet_plane(d, c):
        signal(plane(d))
        return c

    def greet_chip(n, c):
        signal(chip(n))
        return c

    for peer in (phi_low, phi_high, row_low, row_high, band_low, band_high, beyond(1), beyond(7), sibling):
        signal(peer)
    lax.fori_loop(1, 16, greet_chip, 0)
    lax.fori_loop(1, 8, greet_plane, 0)

    for c in loads:
        c.wait()
    for f in range(4):
        for g in range(4):
            src = rho_ref[:, 8 * g : 8 * g + 8, :] if f == 0 else vel_ref[f - 1, :, 8 * g : 8 * g + 8, :]
            t = src.reshape(128, 128).T
            pad[f, g, 8:136, :] = t
            edge[0, pl.ds(f * 4 + g, 1), :] = t[0:1, :]
            edge[1, pl.ds(f * 4 + g, 1), :] = t[127:128, :]
    pl.semaphore_wait(pltpu.get_barrier_semaphore(), 31)
    copies = [
        remote(rho_ref.at[15], hphi.at[0, 0], es.at[0], er.at[0], phi_high),
        remote(vel_ref.at[:, 15], hphi.at[0, pl.ds(1, 3)], es.at[1], er.at[1], phi_high),
        remote(rho_ref.at[0], hphi.at[1, 0], es.at[2], er.at[2], phi_low),
        remote(vel_ref.at[:, 0], hphi.at[1, pl.ds(1, 3)], es.at[3], er.at[3], phi_low),
        remote(edge.at[1], hr.at[0], es.at[4], er.at[4], row_high),
        remote(edge.at[0], hr.at[1], es.at[5], er.at[5], row_low),
    ]
    for c in copies:
        c.start()
    for i, d in enumerate((1, 2, 2)):
        for peer in (beyond(d), beyond(8 - d)):
            pl.semaphore_signal(word.at[i], inc=1, device_id=peer, device_id_type=MESH)
        pl.semaphore_wait(word.at[i], 2)
    for c in copies:
        c.wait()
    has_low = jnp.where(row > 0, 1.0, 0.0)
    has_high = jnp.where(row < 3, 1.0, 0.0)
    for pair in range(2):
        ht[pair] = jnp.concatenate([hphi[s, 2 * pair + f] for f in range(2) for s in range(2)], axis=0).T
    for f in range(4):
        for g in range(4):
            pad[f, g, 7:8, :] = hr[0, pl.ds(f * 4 + g, 1), :] * has_low
            pad[f, g, 136:137, :] = hr[1, pl.ds(f * 4 + g, 1), :] * has_high

    lane = lanes()
    lane8 = lane % 8
    first, last = lane < 8, lane >= 120
    low_th, high_th = lane8 == 0, lane8 == 7
    zero = jnp.zeros((8, 128), F32)

    def band_at(i):
        return lax.rem(z + spread(i // 2), 8) + 8 * (i % 2)

    def spot(i, g):
        j = band_at(i)
        return lax.rem(j, 8) * 8 + g * 2 + j // 8

    own = pltpu.make_async_copy(stepped.at[phi], cyc.at[phi], ls.at[0])

    def send_tiles(i):
        for g in range(4):
            d = spot(i, g)

            @pl.when(d != phi)
            def _():
                remote(stepped.at[d], cyc.at[phi], as_, ar, {"phi": d}).start()

            @pl.when(d == phi)
            def _():
                own.start()

    def step(i, carry):
        base = pl.multiple_of(8 * band_at(i), 8)
        here = [[pad[f, g, pl.ds(base + 8, 8), :] for f in range(4)] for g in range(4)]
        side_edge = [ht[pair, pl.ds(base, 8), :] for pair in range(2)]
        for g in range(4):
            c = here[g]
            before = [pad[f, g, pl.ds(base, 16), :][7:15] for f in range(4)]
            after = [pad[f, g, pl.ds(base + 8, 16), :][1:9] for f in range(4)]
            below = [pltpu.roll(here[g - 1][f], 121, 1) if g > 0 else zero for f in range(4)]
            above = [pltpu.roll(here[g + 1][f], 7, 1) if g < 3 else zero for f in range(4)]
            thm = [jnp.where(low_th, lo, t) for lo, t in zip(below, rolled(c, 1))]
            thp = [jnp.where(high_th, hi, t) for hi, t in zip(above, rolled(c, 127))]
            offs = [(f % 2) * 64 + g * 8 for f in range(4)]
            below = [pltpu.roll(side_edge[f // 2], (128 - offs[f]) % 128, 1) for f in range(4)]
            above = [pltpu.roll(side_edge[f // 2], (120 - offs[f] - 32) % 128, 1) for f in range(4)]
            phm = [jnp.where(first, lo, t) for lo, t in zip(below, rolled(c, 8))]
            php = [jnp.where(last, hi, t) for hi, t in zip(above, rolled(c, 120))]
            new = updated(c, ((2, phm), (3, thm), (1, before)), ((2, php), (3, thp), (1, after)))
            d = spot(i, g)
            for f in range(4):
                stepped[d, f] = new[f]

        @pl.when(i > 0)
        def _():
            send_tiles(i - 1)

        return carry

    lax.fori_loop(0, 16, step, 0)
    send_tiles(15)

    local = z + 8 * y
    shift = shift_ref[local]
    w = frac_ref[local]
    whole, remain = shift // 16, shift % 16
    one, two = 8 * remain, 8 * (remain + 1)
    two_roll = lax.rem(two, 128)
    keep_one, keep_two = lane >= one, lane >= two

    def turn(tiles):
        return rolled(tiles, one) + rolled(tiles, two_roll)

    def blend(cur, prev):
        out = []
        for f in range(4):
            lead = jnp.where(keep_one, cur[f], prev[f])
            trail = jnp.where(keep_two, cur[4 + f], prev[4 + f])
            out.append((1.0 - w) * lead + w * trail)
        return out

    def cycle_slab(p):
        slab = lax.rem(p + 128 - whole, 64)
        return turn([cyc[slab, f] for f in range(4)])

    def move(big, prev):
        top, bottom = [None] * 4, [None] * 4
        for j in range(8):
            cur = cycle_slab(big * 8 + j)
            out = blend(cur, prev)
            prev = cur
            hi, lo = rolled(out, (j - 7) % 128), rolled(out, j) if j else out
            for f in range(4):
                t = out[f]
                t1[big * 8 + j, f] = t
                top[f] = hi[f] if j == 0 else jnp.where(lane8 == j, hi[f], top[f])
                bottom[f] = lo[f] if j == 0 else jnp.where(lane8 == j, lo[f], bottom[f])
                r_edge[0, big * 8 + j, pl.ds(f, 1), :] = t[0:1, :]
                r_edge[1, big * 8 + j, pl.ds(f, 1), :] = t[7:8, :]
        for f in range(4):
            th_edge[0, big, f] = bottom[f]
            th_edge[1, big, f] = top[f]

        @pl.when((big > 0) & (big % 2 == 0))
        def _():
            for c in edge_copies(big // 2 - 1, 1):
                c.start()

        return prev

    def edge_copies(piece, count):
        slabs, groups = pl.ds(piece * 16, 16 * count), pl.ds(piece * 2, 2 * count)
        return [
            remote(r_edge.at[1, slabs], hr2.at[0, slabs], bs.at[0], br.at[0], band_high),
            remote(r_edge.at[0, slabs], hr2.at[1, slabs], bs.at[1], br.at[1], band_low),
            remote(th_edge.at[1, groups], hth.at[0, groups], bs.at[2], br.at[2], group_high),
            remote(th_edge.at[0, groups], hth.at[1, groups], bs.at[3], br.at[3], group_low),
        ]

    pixel = (phi * 4 + row) * 4 + lax.broadcasted_iota(jnp.int32, (8, 1024), 0) % 4
    column = lax.broadcasted_iota(jnp.int32, (8, 1024), 1)
    yy = (pixel.astype(F32) + 0.5) / NPIX * 2.0 - 1.0
    xx = (column.astype(F32) + 0.5) / NPIX * 2.0 - 1.0
    dist = jnp.sqrt(xx * xx + yy * yy)
    u_ref[...] = (dist - R_INNER) / (1.0 - R_INNER) * NR - 0.5
    v_ref[...] = (jnp.arctan2(yy, xx) + jnp.pi) / (2.0 * jnp.pi) * NPHI - 0.5

    wait_all(cyc.at[pl.ds(0, 63)], (as_, ar))
    own.wait()
    lax.fori_loop(0, 8, move, cycle_slab(-1))
    for c in edge_copies(3, 1):
        c.start()
    for c in edge_copies(0, 4):
        c.wait()
    for side_of, cond in enumerate((band > 0, band < 63)):
        hr2[side_of] = hr2[side_of] * jnp.where(cond, 1.0, 0.0)
    for side_of, cond in enumerate((x > 0, x < 3)):
        hth[side_of] = hth[side_of] * jnp.where(cond, 1.0, 0.0)

    sub = lax.broadcasted_iota(jnp.int32, (8, 128), 0)
    low_r, high_r = sub == 0, sub == 7

    def at_slab(p):
        return lax.rem(p + 192 - whole, 64)

    def enter(p):
        here = [t1[at_slab(p), f] for f in range(4)]
        behind = rolled([t1[at_slab(p - 1), f] for f in range(4)], 8)
        return here, behind, rolled(here, 120)

    def hydro_slab(p, window):
        c, phm_far, c_up = window
        q = at_slab(p)
        big, j = q // 8, lax.rem(q, 8)
        ahead = [t1[at_slab(p + 1), f] for f in range(4)]
        ahead_up, c_on = rolled(ahead, 120), rolled(c, 8)
        phm = [jnp.where(first, a, b) for a, b in zip(phm_far, c_on)]
        php = [jnp.where(last, a, b) for a, b in zip(ahead_up, c_up)]
        below = rolled([hth[0, big, f] for f in range(4)], lax.rem(128 - j, 128))
        above = rolled([hth[1, big, f] for f in range(4)], 7 - j)
        thm = [jnp.where(low_th, a, b) for a, b in zip(below, rolled(c, 1))]
        thp = [jnp.where(high_th, a, b) for a, b in zip(above, rolled(c, 127))]
        below = [jnp.broadcast_to(hr2[0, q, pl.ds(f, 1), :], (8, 128)) for f in range(4)]
        above = [jnp.broadcast_to(hr2[1, q, pl.ds(f, 1), :], (8, 128)) for f in range(4)]
        rm = [jnp.where(low_r, a, b) for a, b in zip(below, rolled(c, 1, 0))]
        rp = [jnp.where(high_r, a, b) for a, b in zip(above, rolled(c, 7, 0))]
        new = updated(c, ((2, phm), (3, thm), (1, rm)), ((2, php), (3, thp), (1, rp)))
        return turn(new), (ahead, c_on, ahead_up)

    def rho_message(p):
        return remote(fin.at[p, 0], rho_back.at[phi], rs, rr, {"phi": p})

    def vel_message(p):
        return remote(fin.at[p, pl.ds(1, 3)], back.at[phi], vs, vr, {"phi": p})

    own_rho = pltpu.make_async_copy(fin.at[phi, 0], rho_back.at[phi], ls.at[1])
    own_vel = pltpu.make_async_copy(fin.at[phi, pl.ds(1, 3)], back.at[phi], ls.at[2])

    def send_far(zoff, message):
        def one_slab(i, c):
            message(lax.rem(z + zoff, 8) * 8 + i).start()
            return c

        lax.fori_loop(0, 8, one_slab, 0, unroll=2)

    def send(zoff, message, own_message):
        def one_slab(i, c):
            p = lax.rem(z + zoff, 8) * 8 + i

            @pl.when(p != phi)
            def _():
                message(p).start()

            @pl.when(p == phi)
            def _():
                own_message.start()

            return c

        lax.fori_loop(0, 8, one_slab, 0)

    def block(i, carry):
        start = lax.rem(z + spread(i), 8) * 8

        def slab(k, carry):
            prev, window = carry
            cur, window = hydro_slab(start + k, window)
            out = blend(cur, prev)
            for f in range(4):
                fin[start + k, f] = out[f]
            return cur, window

        lax.fori_loop(0, 8, slab, hydro_slab(start - 1, enter(start - 1)), unroll=UNROLL)

        @pl.when(i > 0)
        def _():
            send_far(spread(i - 1), rho_message)

        @pl.when(i == 5)
        def _():
            send_far(4, vel_message)

        return carry

    lax.fori_loop(0, 8, block, 0)
    send(0, rho_message, own_rho)
    send_far(1, vel_message)
    send_far(7, vel_message)
    send(0, vel_message, own_vel)

    wait_all(rho_back.at[pl.ds(0, 63)], (rs, rr))
    own_rho.wait()
    for g in range(4):
        t = jnp.concatenate([rho_back[where_of(j, g)] for j in range(16)], axis=0).T.reshape(16, 8, 128)
        for i in range(16):
            flat[pl.ds(i * 32 + 8 * g, 8), :] = t[i]
    k = row * 128 + lax.broadcasted_iota(jnp.int32, (16, 128), 1)
    radius = R_INNER + (k.astype(F32) + 0.5) * (1.0 - R_INNER) / NR
    seen = jnp.ones((16, 128), F32)
    total = jnp.zeros((16, 128), F32)
    for j in range(NTH):
        tilt = float(np.float32(1.0 + 0.5 * np.cos(np.pi * (j + 0.5) / NTH)))
        t = jnp.exp(flat[pl.ds(j, 16, stride=32), :] * (-KAPPA / NTH))
        total = total + tilt * ((1.0 - t) * seen)
        seen = seen * t
    light[...] = (1.0 / jnp.sqrt(radius)) * total

    own_light = pltpu.make_async_copy(light, table.at[row, xy, zl], ls.at[3])
    own_light.start()

    def up(n):
        to = {"phi": (half * 4 + lax.rem(zl + n, 4)) * 8 + xy}
        return remote(light, table.at[row, xy, zl], us.at[n], ur.at[n], to)

    def over(n, end):
        to = {"phi": ((1 - half) * 4 + lax.rem(zl + n, 4)) * 8 + xy}
        return remote(light, table.at[row, 8, end], us.at[4 + n], ur.at[4 + n], to)

    ends = ((1, 0, 0), (0, 7, 3))
    for n in (2, 1, 3):
        up(n).start()
    for end, at, plane in ends:

        @pl.when((xy == at) & (zl == plane))
        def _(end=end):
            for n in range(4):
                over(n, end).start()

    for off in (3, 5, 2, 6):
        send_far(off, vel_message)
    for n in (1, 2, 3):
        up(n).wait()
    own_light.wait()
    for end, at, plane in ends:

        @pl.when((xy == at) & (zl == plane))
        def _(end=end):
            for n in range(4):
                over(n, end).wait_send()

        for pos in range(4):

            @pl.when((xy == at) & (zl == pos))
            def _(end=end, pos=pos, plane=plane):
                over((pos - plane) % 4, end).wait_recv()

    def part(q, pos, ssem, rsem, to):
        return remote(table.at[q, pos], table.at[q, pos], ssem, rsem, to)

    def outer(q, end, ssem, rsem, to):
        return remote(table.at[q, 8, end], table.at[q, 8, end], ssem, rsem, to)

    def to_chip(n, c):
        part(row, xy, ps.at[n], pr.at[n], chip(n)).start()
        for end, at, _ in ends:

            @pl.when(xy == at)
            def _(end=end):
                outer(row, end, hs.at[n], hrr.at[n], chip(n)).start()

        return c

    def give(q, pos, n):
        part(q, pos, gs.at[n], gr.at[n], sibling).start()
        for end, at, _ in ends:

            @pl.when(pos == at)
            def _(end=end):
                outer(q, end, hs.at[16 + n], hrr.at[16 + n], sibling).start()

    def source(n):
        m = lax.rem(xy * 2 + yh + 16 - n, 16)
        return m // 2, lax.rem(m, 2)

    def from_chip(n, c):
        pos, high = source(n)
        q = high * 2 + core
        part(q, pos, ps.at[n], pr.at[n], chip(n)).wait_recv()
        for end, at, _ in ends:

            @pl.when(pos == at)
            def _(end=end):
                outer(q, end, hs.at[n], hrr.at[n], chip(n)).wait_recv()

        give(q, pos, n)
        return c

    def finish(n, c):
        pos, high = source(n)
        q, other = high * 2 + core, high * 2 + 1 - core
        part(q, pos, gs.at[n], gr.at[n], sibling).wait_send()
        part(other, pos, gs.at[n], gr.at[n], sibling).wait_recv()
        for end, at, _ in ends:

            @pl.when(pos == at)
            def _(end=end):
                outer(q, end, hs.at[16 + n], hrr.at[16 + n], sibling).wait_send()
                outer(other, end, hs.at[16 + n], hrr.at[16 + n], sibling).wait_recv()

        return c

    def sent(n, c):
        part(row, xy, ps.at[n], pr.at[n], chip(n)).wait_send()
        for end, at, _ in ends:

            @pl.when(xy == at)
            def _(end=end):
                outer(row, end, hs.at[n], hrr.at[n], chip(n)).wait_send()

        return c

    lax.fori_loop(1, 16, to_chip, 0)
    give(row, xy, 0)
    lax.fori_loop(1, 16, from_chip, 0)
    lax.fori_loop(0, 16, finish, 0)
    lax.fori_loop(1, 16, sent, 0)
    wait_all(back.at[pl.ds(0, 63)], (vs, vr))
    own_vel.wait()


@functools.lru_cache(maxsize=None)
def sample_plan(rows_dev):
    yy = ((np.arange(NPIX) + 0.5) / NPIX * 2.0 - 1.0)[:, None]
    xx = ((np.arange(NPIX) + 0.5) / NPIX * 2.0 - 1.0)[None, :]
    u = (np.sqrt(xx * xx + yy * yy) - R_INNER) / (1.0 - R_INNER) * NR - 0.5
    v = (np.arctan2(yy, xx) + np.pi) / (2.0 * np.pi) * NPHI - 0.5
    blocks = NPIX // rows_dev
    plans = []
    for b in range(blocks):
        plan = []
        for c in range(NPIX // 128):
            cut = np.s_[b * rows_dev : (b + 1) * rows_dev, c * 128 : (c + 1) * 128]
            uu, vv = u[cut], v[cut]
            for q in range(NR // 128):
                hit = (uu > q * 128 - 1.01) & (uu < q * 128 + 128.01)
                if hit.any():
                    lo = int(np.floor((vv[hit].min() - 0.01) / 8))
                    hi = int(np.floor((np.floor(vv[hit].max() + 0.01) + 1) / 8))
                    plan.append((c, q, lo, hi - lo + 1))
        plans.append(plan)
    most = max(len(p) for p in plans)
    table = np.zeros((blocks, most, 4), np.int32)
    for b, plan in enumerate(plans):
        table[b, : len(plan)] = plan
    return table


def last_kernel(plan_ref, u_ref, v_ref, rho_src, vel_src, w_ref, rho_ref, vel_ref, out_ref, acc, *, most):
    phi, row = lax.axis_index("phi"), lax.axis_index("row")
    for f in range(4):
        for g in range(4):
            x = jnp.concatenate(
                [rho_src[where_of(j, g)] if f == 0 else vel_src[where_of(j, g), f - 1] for j in range(16)], axis=0
            )
            t = x.T.reshape(16, 8, 128)
            if f == 0:
                rho_ref[:, 8 * g : 8 * g + 8, :] = t
            else:
                vel_ref[f - 1, :, 8 * g : 8 * g + 8, :] = t
    spot = phi * 4 + row
    first_tile = phi // 32 * 64
    acc[...] = jnp.zeros_like(acc)
    sub = lax.broadcasted_iota(jnp.int32, (8, 128), 0)

    def task(t, carry):
        word = plan_ref[spot * most + t]
        chunk, q = word % 8, word // 8 % 4
        lo, count = word // 32 % 256 - 1, word // 8192
        cols = pl.ds(pl.multiple_of(chunk * 128, 128), 128)
        u, v = u_ref[:, cols], v_ref[:, cols]
        floor = jnp.floor(u)
        part = u - floor
        k = floor.astype(jnp.int32) - q * 128 + jnp.where(sub >= 4, 1, 0)
        weight = jnp.where(sub >= 4, part, 1.0 - part)
        weight = jnp.where((k >= 0) & (k < 128), weight, 0.0)
        k = jnp.clip(k, 0, 127)

        def tile(near, total):
            shifted = v - ((near + first_tile) * 8).astype(F32)
            slab = jnp.where(near < 0, 32, jnp.where(near > 63, 33, near // 2 % 8 * 4 + near // 16))
            start = pl.multiple_of(slab * 16 + (near + 2) % 2 * 8, 8)
            for s in range(8):
                line = jnp.broadcast_to(w_ref[q, pl.ds(start + s, 1), :], (8, 128))
                got = jnp.take_along_axis(line, k, axis=1, mode="promise_in_bounds")
                total = total + jnp.maximum(1.0 - jnp.abs(shifted - float(s)), 0.0) * got
            return total

        def pair(i, totals):
            near = lo - first_tile + 4 * i
            return tuple(tile(near + i, t) for i, t in enumerate(totals))

        nothing = jnp.zeros((8, 128), F32)
        a, b, c, d = lax.fori_loop(0, (count + 3) // 4, pair, (nothing,) * 4)
        total = (a + b) + (c + d)
        acc[:, cols] = acc[:, cols] + weight * total
        return carry

    lax.fori_loop(0, most, task, 0)
    out_ref[...] = acc[0:4, :] + acc[4:8, :]


def body(density, velocity, shifts, fractions):
    sds = lambda *s: jax.ShapeDtypeStruct(s, F32)
    dma = lambda *s: pltpu.SemaphoreType.DMA(s)
    vmem = lambda *s: pltpu.VMEM(s, F32)
    one = pltpu.SemaphoreType.DMA
    back, table, rho_back, upos, vpos = pl.pallas_call(
        main_kernel, name="main", out_shape=(sds(64, 3, 8, 128), sds(4, 9, 4, 16, 128), sds(64, 8, 128), sds(8, 1024), sds(8, 1024)),
        in_specs=[SM, SM, ANY, ANY], out_specs=(ANY, ANY, VM, VM, VM),
        scratch_shapes=[
            vmem(16, 32, 128), vmem(3, 16, 32, 128), vmem(4, 4, 144, 128), vmem(2, 16, 128), vmem(2, 4, 32, 128), vmem(2, 16, 128), vmem(2, 128, 128),
            vmem(64, 4, 8, 128), vmem(64, 4, 8, 128), vmem(64, 4, 8, 128),
            vmem(2, 8, 4, 8, 128), vmem(2, 64, 4, 128), vmem(2, 8, 4, 8, 128), vmem(2, 64, 4, 128),
            vmem(64, 4, 8, 128), vmem(512, 128), vmem(16, 128),
            pltpu.SemaphoreType.REGULAR((3,)), dma(6), dma(6), one, one, dma(4), dma(4), one, one, one, one, dma(6), dma(8), dma(8),
            dma(32), dma(32), dma(16), dma(16), dma(16), dma(16),
        ],
        compiler_params=pltpu.CompilerParams(collective_id=0, has_side_effects=True),
    )(shifts, fractions, density, velocity)
    plan = sample_plan(4)
    most = plan.shape[1]
    words = plan[..., 0] + 8 * plan[..., 1] + 32 * (plan[..., 2] + 1) + 8192 * plan[..., 3]
    return pl.pallas_call(
        functools.partial(last_kernel, most=most), name="last",
        out_shape=(sds(16, 32, 128), sds(3, 16, 32, 128), sds(4, 1024)),
        in_specs=[SM, VM, VM, VM, VM, VM], out_specs=(VM, VM, VM),
        scratch_shapes=[pltpu.VMEM((8, 1024), F32)],
    )(jnp.asarray(words.reshape(-1)), upos, vpos, rho_back, back, table.reshape(4, 576, 128))


def solution(mesh):
    in_specs = (P("phi", None, "row"), P(None, "phi", None, "row"), P("row"), P("row"))
    out_specs = (P("phi", None, "row"), P(None, "phi", None, "row"), P(("phi", "row"), None))
    return jax.shard_map(body, mesh=mesh, in_specs=in_specs, out_specs=out_specs, check_vma=False)
```

```python
import functools

import jax
import jax.numpy as jnp
import numpy as np
from jax import lax
from jax.experimental import pallas as pl
from jax.experimental.pallas import tpu as pltpu
from jax.sharding import PartitionSpec as P

MESH = pl.DeviceIdType.MESH
BAND = 8
NPIX = 1024
NPHI = 1024
NR = 512
NTH = 32
UNROLL = 4
KAPPA = 1.5
R_INNER = 0.2
F32 = jnp.float32
VM = pl.BlockSpec(memory_space=pltpu.VMEM)
SM = pl.BlockSpec(memory_space=pltpu.SMEM)
ANY = pl.BlockSpec(memory_space=pl.ANY)


def where_of(band, group):
    return (band % 8) * 8 + group * 2 + band // 8


def lanes():
    return lax.broadcasted_iota(jnp.int32, (8, 128), 1)


def rolled(tiles, by, axis=1):
    return [pltpu.roll(t, by, axis) for t in tiles]


def conserved(q):
    return [q[0], q[0] * q[1], q[0] * q[2], q[0] * q[3]]


def side(q, comp, offset):
    m = q[0] * (0.5 * q[comp] + offset)
    out = [m, m * q[1], m * q[2], m * q[3]]
    out[comp] = out[comp] + 0.5 * q[0]
    return out


def pushed(here, lower, upper):
    total = None
    for (comp, low), (_, high) in zip(lower, upper):
        p, m = side(low, comp, 0.75), side(high, comp, -0.75)
        part = [b - a for a, b in zip(p, m)]
        total = part if total is None else [s + t for s, t in zip(total, part)]
    return [0.775 * c - 0.05 * t for c, t in zip(conserved(here), total)]


def primitive(new):
    inv = 1.0 / new[0]
    return [new[0], new[1] * inv, new[2] * inv, new[3] * inv]


def spread(i):
    return jnp.where(i % 2 == 0, 4 + i // 2, 4 - (i + 1) // 2)


def signal(peer):
    pl.semaphore_signal(pltpu.get_barrier_semaphore(), inc=1, device_id=peer, device_id_type=MESH)


def remote(src, dst, ssem, rsem, to):
    return pltpu.make_async_remote_copy(src, dst, ssem, rsem, device_id=to, device_id_type=MESH)


def wait_all(ref, sems):
    for sem in sems:
        pltpu.make_async_copy(ref, ref, sem).wait()


def main_kernel(
    shift_ref, frac_ref, rho_in, vel_in, back, table, rho_back, u_ref, v_ref,
    rho_ref, vel_ref, pad, edge, hphi, hr, ht, stepped, cyc, t1, th_edge, r_edge, hth, hr2, fin, flat, light,
    word, es, er, as_, ar, bs, br, rs, rr, vs, vr, ls, us, ur, hs, hrr, ps, pr, gs, gr,
):
    phi, row = lax.axis_index("phi"), lax.axis_index("row")
    z, x, y = phi // 8, lax.rem(phi // 2, 4), lax.rem(phi, 2)
    half, zl, xy = z // 4, lax.rem(z, 4), lax.rem(phi, 8)
    core, yh = lax.rem(row, 2), row // 2
    band = row * 16 + y * 8 + z

    def at_band(b):
        j = lax.rem(b, 16)
        return {"phi": lax.rem(j, 8) * 8 + x * 2 + j // 8, "row": b // 16}

    def at_group(g):
        return {"phi": z * 8 + g * 2 + y}

    def chip(n):
        m = lax.rem(xy * 2 + yh + n, 16)
        return {"phi": z * 8 + m // 2, "row": lax.rem(m, 2) * 2 + core}

    sibling = {"row": yh * 2 + 1 - core}
    phi_low, phi_high = {"phi": lax.rem(phi + 63, 64)}, {"phi": lax.rem(phi + 1, 64)}
    row_low, row_high = {"row": lax.rem(row + 3, 4)}, {"row": lax.rem(row + 1, 4)}
    band_low, band_high = at_band(lax.rem(band + 63, 64)), at_band(lax.rem(band + 1, 64))
    group_low, group_high = at_group(lax.rem(x + 3, 4)), at_group(lax.rem(x + 1, 4))

    loads = [
        pltpu.make_async_copy(rho_in, rho_ref, ls.at[4]),
        pltpu.make_async_copy(vel_in, vel_ref, ls.at[5]),
    ]
    for c in loads:
        c.start()

    def plane(d):
        return {"phi": z * 8 + lax.rem(xy + d, 8)}

    def beyond(d):
        return {"phi": lax.rem(z + d, 8) * 8 + xy}

    def greet_plane(d, c):
        signal(plane(d))
        return c

    def greet_chip(n, c):
        signal(chip(n))
        return c

    for peer in (phi_low, phi_high, row_low, row_high, band_low, band_high, beyond(1), beyond(7), sibling):
        signal(peer)
    lax.fori_loop(1, 16, greet_chip, 0)
    lax.fori_loop(1, 8, greet_plane, 0)

    for c in loads:
        c.wait()
    for f in range(4):
        for g in range(4):
            src = rho_ref[:, 8 * g : 8 * g + 8, :] if f == 0 else vel_ref[f - 1, :, 8 * g : 8 * g + 8, :]
            t = src.reshape(128, 128).T
            pad[f, g, 8:136, :] = t
            edge[0, pl.ds(f * 4 + g, 1), :] = t[0:1, :]
            edge[1, pl.ds(f * 4 + g, 1), :] = t[127:128, :]
    pl.semaphore_wait(pltpu.get_barrier_semaphore(), 31)
    copies = [
        remote(rho_ref.at[15], hphi.at[0, 0], es.at[0], er.at[0], phi_high),
        remote(vel_ref.at[:, 15], hphi.at[0, pl.ds(1, 3)], es.at[1], er.at[1], phi_high),
        remote(rho_ref.at[0], hphi.at[1, 0], es.at[2], er.at[2], phi_low),
        remote(vel_ref.at[:, 0], hphi.at[1, pl.ds(1, 3)], es.at[3], er.at[3], phi_low),
        remote(edge.at[1], hr.at[0], es.at[4], er.at[4], row_high),
        remote(edge.at[0], hr.at[1], es.at[5], er.at[5], row_low),
    ]
    for c in copies:
        c.start()
    for i, d in enumerate((1, 2, 2)):
        for peer in (beyond(d), beyond(8 - d)):
            pl.semaphore_signal(word.at[i], inc=1, device_id=peer, device_id_type=MESH)
        pl.semaphore_wait(word.at[i], 2)
    for c in copies:
        c.wait()
    has_low = jnp.where(row > 0, 1.0, 0.0)
    has_high = jnp.where(row < 3, 1.0, 0.0)
    for pair in range(2):
        ht[pair] = jnp.concatenate([hphi[s, 2 * pair + f] for f in range(2) for s in range(2)], axis=0).T
    for f in range(4):
        for g in range(4):
            pad[f, g, 7:8, :] = hr[0, pl.ds(f * 4 + g, 1), :] * has_low
            pad[f, g, 136:137, :] = hr[1, pl.ds(f * 4 + g, 1), :] * has_high

    lane = lanes()
    lane8 = lane % 8
    first, last = lane < 8, lane >= 120
    low_th, high_th = lane8 == 0, lane8 == 7
    zero = jnp.zeros((8, 128), F32)

    def band_at(i):
        return lax.rem(z + spread(i // 2), 8) + 8 * (i % 2)

    def spot(i, g):
        j = band_at(i)
        return lax.rem(j, 8) * 8 + g * 2 + j // 8

    own = pltpu.make_async_copy(stepped.at[phi], cyc.at[phi], ls.at[0])

    def send_tiles(i):
        for g in range(4):
            d = spot(i, g)

            @pl.when(d != phi)
            def _():
                remote(stepped.at[d], cyc.at[phi], as_, ar, {"phi": d}).start()

            @pl.when(d == phi)
            def _():
                own.start()

    def step(i, carry):
        base = pl.multiple_of(8 * band_at(i), 8)
        here = [[pad[f, g, pl.ds(base + 8, 8), :] for f in range(4)] for g in range(4)]
        side_edge = [ht[pair, pl.ds(base, 8), :] for pair in range(2)]
        for g in range(4):
            c = here[g]
            before = [pad[f, g, pl.ds(base, 16), :][7:15] for f in range(4)]
            after = [pad[f, g, pl.ds(base + 8, 16), :][1:9] for f in range(4)]
            below = [pltpu.roll(here[g - 1][f], 121, 1) if g > 0 else zero for f in range(4)]
            above = [pltpu.roll(here[g + 1][f], 7, 1) if g < 3 else zero for f in range(4)]
            thm = [jnp.where(low_th, lo, t) for lo, t in zip(below, rolled(c, 1))]
            thp = [jnp.where(high_th, hi, t) for hi, t in zip(above, rolled(c, 127))]
            offs = [(f % 2) * 64 + g * 8 for f in range(4)]
            below = [pltpu.roll(side_edge[f // 2], (128 - offs[f]) % 128, 1) for f in range(4)]
            above = [pltpu.roll(side_edge[f // 2], (120 - offs[f] - 32) % 128, 1) for f in range(4)]
            phm = [jnp.where(first, lo, t) for lo, t in zip(below, rolled(c, 8))]
            php = [jnp.where(last, hi, t) for hi, t in zip(above, rolled(c, 120))]
            new = primitive(pushed(c, ((2, phm), (3, thm), (1, before)), ((2, php), (3, thp), (1, after))))
            d = spot(i, g)
            for f in range(4):
                stepped[d, f] = new[f]

        @pl.when(i > 0)
        def _():
            send_tiles(i - 1)

        return carry

    lax.fori_loop(0, 16, step, 0)
    send_tiles(15)

    local = z + 8 * y
    shift = shift_ref[local]
    w = frac_ref[local]
    whole, remain = shift // 16, shift % 16
    one, two = 8 * remain, 8 * (remain + 1)
    two_roll = lax.rem(two, 128)
    keep_one, keep_two = lane >= one, lane >= two

    def turn(tiles):
        return rolled(tiles, one) + rolled(tiles, two_roll)

    def blend(cur, prev):
        out = []
        for f in range(4):
            lead = jnp.where(keep_one, cur[f], prev[f])
            trail = jnp.where(keep_two, cur[4 + f], prev[4 + f])
            out.append((1.0 - w) * lead + w * trail)
        return out

    def cycle_slab(p):
        slab = lax.rem(p + 128 - whole, 64)
        return turn([cyc[slab, f] for f in range(4)])

    def move(big, prev):
        top, bottom = [None] * 4, [None] * 4
        for j in range(8):
            cur = cycle_slab(big * 8 + j)
            out = blend(cur, prev)
            prev = cur
            hi, lo = rolled(out, (j - 7) % 128), rolled(out, j) if j else out
            for f in range(4):
                t = out[f]
                t1[big * 8 + j, f] = t
                top[f] = hi[f] if j == 0 else jnp.where(lane8 == j, hi[f], top[f])
                bottom[f] = lo[f] if j == 0 else jnp.where(lane8 == j, lo[f], bottom[f])
                r_edge[0, big * 8 + j, pl.ds(f, 1), :] = t[0:1, :]
                r_edge[1, big * 8 + j, pl.ds(f, 1), :] = t[7:8, :]
        for f in range(4):
            th_edge[0, big, f] = bottom[f]
            th_edge[1, big, f] = top[f]

        @pl.when((big > 0) & (big % 2 == 0))
        def _():
            for c in edge_copies(big // 2 - 1, 1):
                c.start()

        return prev

    def edge_copies(piece, count):
        slabs, groups = pl.ds(piece * 16, 16 * count), pl.ds(piece * 2, 2 * count)
        return [
            remote(r_edge.at[1, slabs], hr2.at[0, slabs], bs.at[0], br.at[0], band_high),
            remote(r_edge.at[0, slabs], hr2.at[1, slabs], bs.at[1], br.at[1], band_low),
            remote(th_edge.at[1, groups], hth.at[0, groups], bs.at[2], br.at[2], group_high),
            remote(th_edge.at[0, groups], hth.at[1, groups], bs.at[3], br.at[3], group_low),
        ]

    pixel = (phi * 4 + row) * 4 + lax.broadcasted_iota(jnp.int32, (8, 1024), 0) % 4
    column = lax.broadcasted_iota(jnp.int32, (8, 1024), 1)
    yy = (pixel.astype(F32) + 0.5) / NPIX * 2.0 - 1.0
    xx = (column.astype(F32) + 0.5) / NPIX * 2.0 - 1.0
    dist = jnp.sqrt(xx * xx + yy * yy)
    u_ref[...] = (dist - R_INNER) / (1.0 - R_INNER) * NR - 0.5
    v_ref[...] = (jnp.arctan2(yy, xx) + jnp.pi) / (2.0 * jnp.pi) * NPHI - 0.5

    wait_all(cyc.at[pl.ds(0, 63)], (as_, ar))
    own.wait()
    lax.fori_loop(0, 8, move, cycle_slab(-1))
    for c in edge_copies(3, 1):
        c.start()
    sub = lax.broadcasted_iota(jnp.int32, (8, 128), 0)
    low_r, high_r = sub == 0, sub == 7

    def inside(q, window):
        c, phm_far, c_up = window
        ahead = [t1[lax.rem(q + 1, 64), f] for f in range(4)]
        ahead_up, c_on = rolled(ahead, 120), rolled(c, 8)
        phm = [jnp.where(first, a, b) for a, b in zip(phm_far, c_on)]
        php = [jnp.where(last, a, b) for a, b in zip(ahead_up, c_up)]
        thm = [jnp.where(low_th, 0.0, b) for b in rolled(c, 1)]
        thp = [jnp.where(high_th, 0.0, b) for b in rolled(c, 127)]
        rm = [jnp.where(low_r, 0.0, b) for b in rolled(c, 1, 0)]
        rp = [jnp.where(high_r, 0.0, b) for b in rolled(c, 7, 0)]
        new = pushed(c, ((2, phm), (3, thm), (1, rm)), ((2, php), (3, thp), (1, rp)))
        for f in range(4):
            stepped[q, f] = new[f]
        return ahead, c_on, ahead_up

    here = [t1[0, f] for f in range(4)]
    lax.fori_loop(
        0, 64, inside, (here, rolled([t1[63, f] for f in range(4)], 8), rolled(here, 120)), unroll=UNROLL
    )
    for c in edge_copies(0, 4):
        c.wait()
    for side_of, cond in enumerate((band > 0, band < 63)):
        hr2[side_of] = hr2[side_of] * jnp.where(cond, 1.0, 0.0)
    for side_of, cond in enumerate((x > 0, x < 3)):
        hth[side_of] = hth[side_of] * jnp.where(cond, 1.0, 0.0)

    offset_r, offset_th = jnp.where(low_r, 0.75, -0.75), jnp.where(low_th, 0.75, -0.75)
    weight_r = jnp.where(low_r, 0.05, jnp.where(high_r, -0.05, 0.0))
    weight_th = jnp.where(low_th, 0.05, jnp.where(high_th, -0.05, 0.0))

    def hydro_slab(p):
        q = lax.rem(p + 192 - whole, 64)
        big, j = q // 8, lax.rem(q, 8)
        below = rolled([hth[0, big, f] for f in range(4)], lax.rem(128 - j, 128))
        above = rolled([hth[1, big, f] for f in range(4)], 7 - j)
        add_th = side([jnp.where(low_th, a, b) for a, b in zip(below, above)], 3, offset_th)
        below = [jnp.broadcast_to(hr2[0, q, pl.ds(f, 1), :], (8, 128)) for f in range(4)]
        above = [jnp.broadcast_to(hr2[1, q, pl.ds(f, 1), :], (8, 128)) for f in range(4)]
        add_r = side([jnp.where(low_r, a, b) for a, b in zip(below, above)], 1, offset_r)
        new = [stepped[q, f] + weight_th * add_th[f] + weight_r * add_r[f] for f in range(4)]
        return turn(primitive(new))

    def rho_message(p):
        return remote(fin.at[p, 0], rho_back.at[phi], rs, rr, {"phi": p})

    def vel_message(p):
        return remote(fin.at[p, pl.ds(1, 3)], back.at[phi], vs, vr, {"phi": p})

    own_rho = pltpu.make_async_copy(fin.at[phi, 0], rho_back.at[phi], ls.at[1])
    own_vel = pltpu.make_async_copy(fin.at[phi, pl.ds(1, 3)], back.at[phi], ls.at[2])

    def send_far(zoff, message):
        def one_slab(i, c):
            message(lax.rem(z + zoff, 8) * 8 + i).start()
            return c

        lax.fori_loop(0, 8, one_slab, 0, unroll=2)

    def send(zoff, message, own_message):
        def one_slab(i, c):
            p = lax.rem(z + zoff, 8) * 8 + i

            @pl.when(p != phi)
            def _():
                message(p).start()

            @pl.when(p == phi)
            def _():
                own_message.start()

            return c

        lax.fori_loop(0, 8, one_slab, 0)

    def block(i, carry):
        start = lax.rem(z + spread(i), 8) * 8

        def slab(k, prev):
            cur = hydro_slab(start + k)
            out = blend(cur, prev)
            for f in range(4):
                fin[start + k, f] = out[f]
            return cur

        lax.fori_loop(0, 8, slab, hydro_slab(start - 1), unroll=8)

        @pl.when(i > 0)
        def _():
            send_far(spread(i - 1), rho_message)

        @pl.when(i == 3)
        def _():
            send_far(4, vel_message)

        return carry

    lax.fori_loop(0, 8, block, 0)
    send(0, rho_message, own_rho)
    send_far(1, vel_message)
    send_far(7, vel_message)
    send(0, vel_message, own_vel)

    wait_all(rho_back.at[pl.ds(0, 63)], (rs, rr))
    own_rho.wait()
    for g in range(4):
        t = jnp.concatenate([rho_back[where_of(j, g)] for j in range(16)], axis=0).T.reshape(16, 8, 128)
        for i in range(16):
            flat[pl.ds(i * 32 + 8 * g, 8), :] = t[i]
    k = row * 128 + lax.broadcasted_iota(jnp.int32, (16, 128), 1)
    radius = R_INNER + (k.astype(F32) + 0.5) * (1.0 - R_INNER) / NR
    seen = jnp.ones((16, 128), F32)
    total = jnp.zeros((16, 128), F32)
    for j in range(NTH):
        tilt = float(np.float32(1.0 + 0.5 * np.cos(np.pi * (j + 0.5) / NTH)))
        t = jnp.exp(flat[pl.ds(j, 16, stride=32), :] * (-KAPPA / NTH))
        total = total + tilt * ((1.0 - t) * seen)
        seen = seen * t
    light[...] = (1.0 / jnp.sqrt(radius)) * total

    own_light = pltpu.make_async_copy(light, table.at[row, xy, zl], ls.at[3])
    own_light.start()

    def up(n):
        to = {"phi": (half * 4 + lax.rem(zl + n, 4)) * 8 + xy}
        return remote(light, table.at[row, xy, zl], us.at[n], ur.at[n], to)

    def over(n, end):
        to = {"phi": ((1 - half) * 4 + lax.rem(zl + n, 4)) * 8 + xy}
        return remote(light, table.at[row, 8, end], us.at[4 + n], ur.at[4 + n], to)

    ends = ((1, 0, 0), (0, 7, 3))
    for n in (2, 1, 3):
        up(n).start()
    for end, at, plane in ends:

        @pl.when((xy == at) & (zl == plane))
        def _(end=end):
            for n in range(4):
                over(n, end).start()

    for off in (3, 5, 2, 6):
        send_far(off, vel_message)
    for n in (1, 2, 3):
        up(n).wait()
    own_light.wait()
    for end, at, plane in ends:

        @pl.when((xy == at) & (zl == plane))
        def _(end=end):
            for n in range(4):
                over(n, end).wait_send()

        for pos in range(4):

            @pl.when((xy == at) & (zl == pos))
            def _(end=end, pos=pos, plane=plane):
                over((pos - plane) % 4, end).wait_recv()

    def part(q, pos, ssem, rsem, to):
        return remote(table.at[q, pos], table.at[q, pos], ssem, rsem, to)

    def outer(q, end, ssem, rsem, to):
        return remote(table.at[q, 8, end], table.at[q, 8, end], ssem, rsem, to)

    def to_chip(n, c):
        part(row, xy, ps.at[n], pr.at[n], chip(n)).start()
        for end, at, _ in ends:

            @pl.when(xy == at)
            def _(end=end):
                outer(row, end, hs.at[n], hrr.at[n], chip(n)).start()

        return c

    def give(q, pos, n):
        part(q, pos, gs.at[n], gr.at[n], sibling).start()
        for end, at, _ in ends:

            @pl.when(pos == at)
            def _(end=end):
                outer(q, end, hs.at[16 + n], hrr.at[16 + n], sibling).start()

    def source(n):
        m = lax.rem(xy * 2 + yh + 16 - n, 16)
        return m // 2, lax.rem(m, 2)

    def from_chip(n, c):
        pos, high = source(n)
        q = high * 2 + core
        part(q, pos, ps.at[n], pr.at[n], chip(n)).wait_recv()
        for end, at, _ in ends:

            @pl.when(pos == at)
            def _(end=end):
                outer(q, end, hs.at[n], hrr.at[n], chip(n)).wait_recv()

        give(q, pos, n)
        return c

    def finish(n, c):
        pos, high = source(n)
        q, other = high * 2 + core, high * 2 + 1 - core
        part(q, pos, gs.at[n], gr.at[n], sibling).wait_send()
        part(other, pos, gs.at[n], gr.at[n], sibling).wait_recv()
        for end, at, _ in ends:

            @pl.when(pos == at)
            def _(end=end):
                outer(q, end, hs.at[16 + n], hrr.at[16 + n], sibling).wait_send()
                outer(other, end, hs.at[16 + n], hrr.at[16 + n], sibling).wait_recv()

        return c

    def sent(n, c):
        part(row, xy, ps.at[n], pr.at[n], chip(n)).wait_send()
        for end, at, _ in ends:

            @pl.when(xy == at)
            def _(end=end):
                outer(row, end, hs.at[n], hrr.at[n], chip(n)).wait_send()

        return c

    lax.fori_loop(1, 16, to_chip, 0)
    give(row, xy, 0)
    lax.fori_loop(1, 16, from_chip, 0)
    lax.fori_loop(0, 16, finish, 0)
    lax.fori_loop(1, 16, sent, 0)
    wait_all(back.at[pl.ds(0, 63)], (vs, vr))
    own_vel.wait()


@functools.lru_cache(maxsize=None)
def sample_plan(rows_dev):
    yy = ((np.arange(NPIX) + 0.5) / NPIX * 2.0 - 1.0)[:, None]
    xx = ((np.arange(NPIX) + 0.5) / NPIX * 2.0 - 1.0)[None, :]
    u = (np.sqrt(xx * xx + yy * yy) - R_INNER) / (1.0 - R_INNER) * NR - 0.5
    v = (np.arctan2(yy, xx) + np.pi) / (2.0 * np.pi) * NPHI - 0.5
    blocks = NPIX // rows_dev
    plans = []
    for b in range(blocks):
        plan = []
        for c in range(NPIX // 128):
            cut = np.s_[b * rows_dev : (b + 1) * rows_dev, c * 128 : (c + 1) * 128]
            uu, vv = u[cut], v[cut]
            for q in range(NR // 128):
                hit = (uu > q * 128 - 1.01) & (uu < q * 128 + 128.01)
                if hit.any():
                    lo = int(np.floor((vv[hit].min() - 0.01) / 8))
                    hi = int(np.floor((np.floor(vv[hit].max() + 0.01) + 1) / 8))
                    plan.append((c, q, lo, hi - lo + 1))
        plans.append(plan)
    most = max(len(p) for p in plans)
    table = np.zeros((blocks, most, 4), np.int32)
    for b, plan in enumerate(plans):
        table[b, : len(plan)] = plan
    return table


def last_kernel(plan_ref, u_ref, v_ref, rho_src, vel_src, w_ref, rho_ref, vel_ref, out_ref, acc, *, most):
    phi, row = lax.axis_index("phi"), lax.axis_index("row")
    for f in range(4):
        for g in range(4):
            x = jnp.concatenate(
                [rho_src[where_of(j, g)] if f == 0 else vel_src[where_of(j, g), f - 1] for j in range(16)], axis=0
            )
            t = x.T.reshape(16, 8, 128)
            if f == 0:
                rho_ref[:, 8 * g : 8 * g + 8, :] = t
            else:
                vel_ref[f - 1, :, 8 * g : 8 * g + 8, :] = t
    spot = phi * 4 + row
    first_tile = phi // 32 * 64
    acc[...] = jnp.zeros_like(acc)
    sub = lax.broadcasted_iota(jnp.int32, (8, 128), 0)

    def task(t, carry):
        word = plan_ref[spot * most + t]
        chunk, q = word % 8, word // 8 % 4
        lo, count = word // 32 % 256 - 1, word // 8192
        cols = pl.ds(pl.multiple_of(chunk * 128, 128), 128)
        u, v = u_ref[:, cols], v_ref[:, cols]
        floor = jnp.floor(u)
        part = u - floor
        k = floor.astype(jnp.int32) - q * 128 + jnp.where(sub >= 4, 1, 0)
        weight = jnp.where(sub >= 4, part, 1.0 - part)
        weight = jnp.where((k >= 0) & (k < 128), weight, 0.0)
        k = jnp.clip(k, 0, 127)

        def tile(near, total):
            shifted = v - ((near + first_tile) * 8).astype(F32)
            slab = jnp.where(near < 0, 32, jnp.where(near > 63, 33, near // 2 % 8 * 4 + near // 16))
            start = pl.multiple_of(slab * 16 + (near + 2) % 2 * 8, 8)
            for s in range(8):
                line = jnp.broadcast_to(w_ref[q, pl.ds(start + s, 1), :], (8, 128))
                got = jnp.take_along_axis(line, k, axis=1, mode="promise_in_bounds")
                total = total + jnp.maximum(1.0 - jnp.abs(shifted - float(s)), 0.0) * got
            return total

        def pair(i, totals):
            near = lo - first_tile + 4 * i
            return tuple(tile(near + i, t) for i, t in enumerate(totals))

        nothing = jnp.zeros((8, 128), F32)
        a, b, c, d = lax.fori_loop(0, (count + 3) // 4, pair, (nothing,) * 4)
        total = (a + b) + (c + d)
        acc[:, cols] = acc[:, cols] + weight * total
        return carry

    lax.fori_loop(0, most, task, 0)
    out_ref[...] = acc[0:4, :] + acc[4:8, :]


def body(density, velocity, shifts, fractions):
    sds = lambda *s: jax.ShapeDtypeStruct(s, F32)
    dma = lambda *s: pltpu.SemaphoreType.DMA(s)
    vmem = lambda *s: pltpu.VMEM(s, F32)
    one = pltpu.SemaphoreType.DMA
    back, table, rho_back, upos, vpos = pl.pallas_call(
        main_kernel, name="main", out_shape=(sds(64, 3, 8, 128), sds(4, 9, 4, 16, 128), sds(64, 8, 128), sds(8, 1024), sds(8, 1024)),
        in_specs=[SM, SM, ANY, ANY], out_specs=(ANY, ANY, VM, VM, VM),
        scratch_shapes=[
            vmem(16, 32, 128), vmem(3, 16, 32, 128), vmem(4, 4, 144, 128), vmem(2, 16, 128), vmem(2, 4, 32, 128), vmem(2, 16, 128), vmem(2, 128, 128),
            vmem(64, 4, 8, 128), vmem(64, 4, 8, 128), vmem(64, 4, 8, 128),
            vmem(2, 8, 4, 8, 128), vmem(2, 64, 4, 128), vmem(2, 8, 4, 8, 128), vmem(2, 64, 4, 128),
            vmem(64, 4, 8, 128), vmem(512, 128), vmem(16, 128),
            pltpu.SemaphoreType.REGULAR((3,)), dma(6), dma(6), one, one, dma(4), dma(4), one, one, one, one, dma(6), dma(8), dma(8),
            dma(32), dma(32), dma(16), dma(16), dma(16), dma(16),
        ],
        compiler_params=pltpu.CompilerParams(collective_id=0, has_side_effects=True),
    )(shifts, fractions, density, velocity)
    plan = sample_plan(4)
    most = plan.shape[1]
    words = plan[..., 0] + 8 * plan[..., 1] + 32 * (plan[..., 2] + 1) + 8192 * plan[..., 3]
    return pl.pallas_call(
        functools.partial(last_kernel, most=most), name="last",
        out_shape=(sds(16, 32, 128), sds(3, 16, 32, 128), sds(4, 1024)),
        in_specs=[SM, VM, VM, VM, VM, VM], out_specs=(VM, VM, VM),
        scratch_shapes=[pltpu.VMEM((8, 1024), F32)],
    )(jnp.asarray(words.reshape(-1)), upos, vpos, rho_back, back, table.reshape(4, 576, 128))


def solution(mesh):
    in_specs = (P("phi", None, "row"), P(None, "phi", None, "row"), P("row"), P("row"))
    out_specs = (P("phi", None, "row"), P(None, "phi", None, "row"), P(("phi", "row"), None))
    return jax.shard_map(body, mesh=mesh, in_specs=in_specs, out_specs=out_specs, check_vma=False)
```

```python
import functools

import jax
import jax.numpy as jnp
import numpy as np
from jax import lax
from jax.experimental import pallas as pl
from jax.experimental.pallas import tpu as pltpu
from jax.sharding import PartitionSpec as P

MESH = pl.DeviceIdType.MESH
BAND = 8
NPIX = 1024
NPHI = 1024
NR = 512
NTH = 32
UNROLL = 8
KAPPA = 1.5
R_INNER = 0.2
F32 = jnp.float32
VM = pl.BlockSpec(memory_space=pltpu.VMEM)
SM = pl.BlockSpec(memory_space=pltpu.SMEM)
ANY = pl.BlockSpec(memory_space=pl.ANY)


def where_of(band, group):
    return (band % 8) * 8 + group * 2 + band // 8


def lanes():
    return lax.broadcasted_iota(jnp.int32, (8, 128), 1)


def rolled(tiles, by, axis=1):
    return [pltpu.roll(t, by, axis) for t in tiles]


def conserved(q):
    return [q[0], q[0] * q[1], q[0] * q[2], q[0] * q[3]]


def side(q, comp, offset):
    m = q[0] * (0.5 * q[comp] + offset)
    out = [m, m * q[1], m * q[2], m * q[3]]
    out[comp] = out[comp] + 0.5 * q[0]
    return out


def pushed(here, lower, upper):
    total = None
    for (comp, low), (_, high) in zip(lower, upper):
        p, m = side(low, comp, 0.75), side(high, comp, -0.75)
        part = [b - a for a, b in zip(p, m)]
        total = part if total is None else [s + t for s, t in zip(total, part)]
    return [0.775 * c - 0.05 * t for c, t in zip(conserved(here), total)]


def primitive(new):
    inv = 1.0 / new[0]
    return [new[0], new[1] * inv, new[2] * inv, new[3] * inv]


def spread(i):
    return jnp.where(i % 2 == 0, 4 + i // 2, 4 - (i + 1) // 2)


def signal(peer):
    pl.semaphore_signal(pltpu.get_barrier_semaphore(), inc=1, device_id=peer, device_id_type=MESH)


def remote(src, dst, ssem, rsem, to):
    return pltpu.make_async_remote_copy(src, dst, ssem, rsem, device_id=to, device_id_type=MESH)


def wait_all(ref, sems):
    for sem in sems:
        pltpu.make_async_copy(ref, ref, sem).wait()


def main_kernel(
    shift_ref, frac_ref, rho_in, vel_in, back, table, rho_back, u_ref, v_ref,
    rho_ref, vel_ref, pad, edge, hphi, hr, ht, stepped, cyc, t1, th_edge, r_edge, hth, hr2, fin, flat, light,
    word, es, er, as_, ar, bs, br, rs, rr, vs, vr, ls, us, ur, hs, hrr, ps, pr, gs, gr,
):
    phi, row = lax.axis_index("phi"), lax.axis_index("row")
    z, x, y = phi // 8, lax.rem(phi // 2, 4), lax.rem(phi, 2)
    half, zl, xy = z // 4, lax.rem(z, 4), lax.rem(phi, 8)
    core, yh = lax.rem(row, 2), row // 2
    band = row * 16 + y * 8 + z

    def at_band(b):
        j = lax.rem(b, 16)
        return {"phi": lax.rem(j, 8) * 8 + x * 2 + j // 8, "row": b // 16}

    def at_group(g):
        return {"phi": z * 8 + g * 2 + y}

    def chip(n):
        m = lax.rem(xy * 2 + yh + n, 16)
        return {"phi": z * 8 + m // 2, "row": lax.rem(m, 2) * 2 + core}

    sibling = {"row": yh * 2 + 1 - core}
    phi_low, phi_high = {"phi": lax.rem(phi + 63, 64)}, {"phi": lax.rem(phi + 1, 64)}
    row_low, row_high = {"row": lax.rem(row + 3, 4)}, {"row": lax.rem(row + 1, 4)}
    band_low, band_high = at_band(lax.rem(band + 63, 64)), at_band(lax.rem(band + 1, 64))
    group_low, group_high = at_group(lax.rem(x + 3, 4)), at_group(lax.rem(x + 1, 4))

    loads = [
        pltpu.make_async_copy(rho_in, rho_ref, ls.at[4]),
        pltpu.make_async_copy(vel_in, vel_ref, ls.at[5]),
    ]
    for c in loads:
        c.start()

    def plane(d):
        return {"phi": z * 8 + lax.rem(xy + d, 8)}

    def beyond(d):
        return {"phi": lax.rem(z + d, 8) * 8 + xy}

    def greet_plane(d, c):
        signal(plane(d))
        return c

    def greet_chip(n, c):
        signal(chip(n))
        return c

    for peer in (phi_low, phi_high, row_low, row_high, band_low, band_high, beyond(1), beyond(7), sibling):
        signal(peer)
    lax.fori_loop(1, 16, greet_chip, 0)
    lax.fori_loop(1, 8, greet_plane, 0)

    for c in loads:
        c.wait()
    for f in range(4):
        for g in range(4):
            src = rho_ref[:, 8 * g : 8 * g + 8, :] if f == 0 else vel_ref[f - 1, :, 8 * g : 8 * g + 8, :]
            t = src.reshape(128, 128).T
            pad[f, g, 8:136, :] = t
            edge[0, pl.ds(f * 4 + g, 1), :] = t[0:1, :]
            edge[1, pl.ds(f * 4 + g, 1), :] = t[127:128, :]
    pl.semaphore_wait(pltpu.get_barrier_semaphore(), 31)
    copies = [
        remote(rho_ref.at[15], hphi.at[0, 0], es.at[0], er.at[0], phi_high),
        remote(vel_ref.at[:, 15], hphi.at[0, pl.ds(1, 3)], es.at[1], er.at[1], phi_high),
        remote(rho_ref.at[0], hphi.at[1, 0], es.at[2], er.at[2], phi_low),
        remote(vel_ref.at[:, 0], hphi.at[1, pl.ds(1, 3)], es.at[3], er.at[3], phi_low),
        remote(edge.at[1], hr.at[0], es.at[4], er.at[4], row_high),
        remote(edge.at[0], hr.at[1], es.at[5], er.at[5], row_low),
    ]
    for c in copies:
        c.start()
    for i, d in enumerate((1, 2, 2)):
        for peer in (beyond(d), beyond(8 - d)):
            pl.semaphore_signal(word.at[i], inc=1, device_id=peer, device_id_type=MESH)
        pl.semaphore_wait(word.at[i], 2)
    for c in copies:
        c.wait()
    has_low = jnp.where(row > 0, 1.0, 0.0)
    has_high = jnp.where(row < 3, 1.0, 0.0)
    for pair in range(2):
        ht[pair] = jnp.concatenate([hphi[s, 2 * pair + f] for f in range(2) for s in range(2)], axis=0).T
    for f in range(4):
        for g in range(4):
            pad[f, g, 7:8, :] = hr[0, pl.ds(f * 4 + g, 1), :] * has_low
            pad[f, g, 136:137, :] = hr[1, pl.ds(f * 4 + g, 1), :] * has_high

    lane = lanes()
    lane8 = lane % 8
    first, last = lane < 8, lane >= 120
    low_th, high_th = lane8 == 0, lane8 == 7
    zero = jnp.zeros((8, 128), F32)

    def band_at(i):
        return lax.rem(z + spread(i // 2), 8) + 8 * (i % 2)

    def spot(i, g):
        j = band_at(i)
        return lax.rem(j, 8) * 8 + g * 2 + j // 8

    own = pltpu.make_async_copy(stepped.at[phi], cyc.at[phi], ls.at[0])

    def send_tiles(i):
        for g in range(4):
            d = spot(i, g)

            @pl.when(d != phi)
            def _():
                remote(stepped.at[d], cyc.at[phi], as_, ar, {"phi": d}).start()

            @pl.when(d == phi)
            def _():
                own.start()

    def step(i, carry):
        base = pl.multiple_of(8 * band_at(i), 8)
        here = [[pad[f, g, pl.ds(base + 8, 8), :] for f in range(4)] for g in range(4)]
        side_edge = [ht[pair, pl.ds(base, 8), :] for pair in range(2)]
        for g in range(4):
            c = here[g]
            before = [pad[f, g, pl.ds(base, 16), :][7:15] for f in range(4)]
            after = [pad[f, g, pl.ds(base + 8, 16), :][1:9] for f in range(4)]
            below = [pltpu.roll(here[g - 1][f], 121, 1) if g > 0 else zero for f in range(4)]
            above = [pltpu.roll(here[g + 1][f], 7, 1) if g < 3 else zero for f in range(4)]
            thm = [jnp.where(low_th, lo, t) for lo, t in zip(below, rolled(c, 1))]
            thp = [jnp.where(high_th, hi, t) for hi, t in zip(above, rolled(c, 127))]
            offs = [(f % 2) * 64 + g * 8 for f in range(4)]
            below = [pltpu.roll(side_edge[f // 2], (128 - offs[f]) % 128, 1) for f in range(4)]
            above = [pltpu.roll(side_edge[f // 2], (120 - offs[f] - 32) % 128, 1) for f in range(4)]
            phm = [jnp.where(first, lo, t) for lo, t in zip(below, rolled(c, 8))]
            php = [jnp.where(last, hi, t) for hi, t in zip(above, rolled(c, 120))]
            new = primitive(pushed(c, ((2, phm), (3, thm), (1, before)), ((2, php), (3, thp), (1, after))))
            d = spot(i, g)
            for f in range(4):
                stepped[d, f] = new[f]

        @pl.when(i > 0)
        def _():
            send_tiles(i - 1)

        return carry

    lax.fori_loop(0, 16, step, 0)
    send_tiles(15)

    local = z + 8 * y
    shift = shift_ref[local]
    w = frac_ref[local]
    whole, remain = shift // 16, shift % 16
    one, two = 8 * remain, 8 * (remain + 1)
    two_roll = lax.rem(two, 128)
    keep_one, keep_two = lane >= one, lane >= two

    def turn(tiles):
        return rolled(tiles, one) + rolled(tiles, two_roll)

    def blend(cur, prev):
        out = []
        for f in range(4):
            lead = jnp.where(keep_one, cur[f], prev[f])
            trail = jnp.where(keep_two, cur[4 + f], prev[4 + f])
            out.append((1.0 - w) * lead + w * trail)
        return out

    def cycle_slab(p):
        slab = lax.rem(p + 128 - whole, 64)
        return turn([cyc[slab, f] for f in range(4)])

    def move(big, prev):
        top, bottom = [None] * 4, [None] * 4
        for j in range(8):
            cur = cycle_slab(big * 8 + j)
            out = blend(cur, prev)
            prev = cur
            hi, lo = rolled(out, (j - 7) % 128), rolled(out, j) if j else out
            for f in range(4):
                t = out[f]
                t1[big * 8 + j, f] = t
                top[f] = hi[f] if j == 0 else jnp.where(lane8 == j, hi[f], top[f])
                bottom[f] = lo[f] if j == 0 else jnp.where(lane8 == j, lo[f], bottom[f])
                r_edge[0, big * 8 + j, pl.ds(f, 1), :] = t[0:1, :]
                r_edge[1, big * 8 + j, pl.ds(f, 1), :] = t[7:8, :]
        for f in range(4):
            th_edge[0, big, f] = bottom[f]
            th_edge[1, big, f] = top[f]

        @pl.when((big > 0) & (big % 2 == 0))
        def _():
            for c in edge_copies(big // 2 - 1, 1):
                c.start()

        return prev

    def edge_copies(piece, count):
        slabs, groups = pl.ds(piece * 16, 16 * count), pl.ds(piece * 2, 2 * count)
        return [
            remote(r_edge.at[1, slabs], hr2.at[0, slabs], bs.at[0], br.at[0], band_high),
            remote(r_edge.at[0, slabs], hr2.at[1, slabs], bs.at[1], br.at[1], band_low),
            remote(th_edge.at[1, groups], hth.at[0, groups], bs.at[2], br.at[2], group_high),
            remote(th_edge.at[0, groups], hth.at[1, groups], bs.at[3], br.at[3], group_low),
        ]

    pixel = (phi * 4 + row) * 4 + lax.broadcasted_iota(jnp.int32, (8, 1024), 0) % 4
    column = lax.broadcasted_iota(jnp.int32, (8, 1024), 1)
    yy = (pixel.astype(F32) + 0.5) / NPIX * 2.0 - 1.0
    xx = (column.astype(F32) + 0.5) / NPIX * 2.0 - 1.0
    dist = jnp.sqrt(xx * xx + yy * yy)
    u_ref[...] = (dist - R_INNER) / (1.0 - R_INNER) * NR - 0.5
    v_ref[...] = (jnp.arctan2(yy, xx) + jnp.pi) / (2.0 * jnp.pi) * NPHI - 0.5

    wait_all(cyc.at[pl.ds(0, 63)], (as_, ar))
    own.wait()
    lax.fori_loop(0, 8, move, cycle_slab(-1))
    for c in edge_copies(3, 1):
        c.start()
    sub = lax.broadcasted_iota(jnp.int32, (8, 128), 0)
    low_r, high_r = sub == 0, sub == 7

    def inside(q, window):
        c, phm_far, c_up = window
        ahead = [t1[lax.rem(q + 1, 64), f] for f in range(4)]
        ahead_up, c_on = rolled(ahead, 120), rolled(c, 8)
        phm = [jnp.where(first, a, b) for a, b in zip(phm_far, c_on)]
        php = [jnp.where(last, a, b) for a, b in zip(ahead_up, c_up)]
        thm = [jnp.where(low_th, 0.0, b) for b in rolled(c, 1)]
        thp = [jnp.where(high_th, 0.0, b) for b in rolled(c, 127)]
        rm = [jnp.where(low_r, 0.0, b) for b in rolled(c, 1, 0)]
        rp = [jnp.where(high_r, 0.0, b) for b in rolled(c, 7, 0)]
        new = pushed(c, ((2, phm), (3, thm), (1, rm)), ((2, php), (3, thp), (1, rp)))
        for f in range(4):
            stepped[q, f] = new[f]
        return ahead, c_on, ahead_up

    here = [t1[0, f] for f in range(4)]
    lax.fori_loop(
        0, 64, inside, (here, rolled([t1[63, f] for f in range(4)], 8), rolled(here, 120)), unroll=UNROLL
    )
    for c in edge_copies(0, 4):
        c.wait()
    for side_of, cond in enumerate((band > 0, band < 63)):
        hr2[side_of] = hr2[side_of] * jnp.where(cond, 1.0, 0.0)
    for side_of, cond in enumerate((x > 0, x < 3)):
        hth[side_of] = hth[side_of] * jnp.where(cond, 1.0, 0.0)

    offset_r, offset_th = jnp.where(low_r, 0.75, -0.75), jnp.where(low_th, 0.75, -0.75)
    weight_r = jnp.where(low_r, 0.05, jnp.where(high_r, -0.05, 0.0))
    weight_th = jnp.where(low_th, 0.05, jnp.where(high_th, -0.05, 0.0))

    def hydro_slab(p):
        q = lax.rem(p + 192 - whole, 64)
        big, j = q // 8, lax.rem(q, 8)
        below = rolled([hth[0, big, f] for f in range(4)], lax.rem(128 - j, 128))
        above = rolled([hth[1, big, f] for f in range(4)], 7 - j)
        add_th = side([jnp.where(low_th, a, b) for a, b in zip(below, above)], 3, offset_th)
        below = [jnp.broadcast_to(hr2[0, q, pl.ds(f, 1), :], (8, 128)) for f in range(4)]
        above = [jnp.broadcast_to(hr2[1, q, pl.ds(f, 1), :], (8, 128)) for f in range(4)]
        add_r = side([jnp.where(low_r, a, b) for a, b in zip(below, above)], 1, offset_r)
        new = [stepped[q, f] + weight_th * add_th[f] + weight_r * add_r[f] for f in range(4)]
        return turn(primitive(new))

    def rho_message(p):
        return remote(fin.at[p, 0], rho_back.at[phi], rs, rr, {"phi": p})

    def vel_message(p):
        return remote(fin.at[p, pl.ds(1, 3)], back.at[phi], vs, vr, {"phi": p})

    own_rho = pltpu.make_async_copy(fin.at[phi, 0], rho_back.at[phi], ls.at[1])
    own_vel = pltpu.make_async_copy(fin.at[phi, pl.ds(1, 3)], back.at[phi], ls.at[2])

    def send_far(zoff, message):
        def one_slab(i, c):
            message(lax.rem(z + zoff, 8) * 8 + i).start()
            return c

        lax.fori_loop(0, 8, one_slab, 0, unroll=2)

    def send(zoff, message, own_message):
        def one_slab(i, c):
            p = lax.rem(z + zoff, 8) * 8 + i

            @pl.when(p != phi)
            def _():
                message(p).start()

            @pl.when(p == phi)
            def _():
                own_message.start()

            return c

        lax.fori_loop(0, 8, one_slab, 0)

    def block(i, carry):
        start = lax.rem(z + spread(i), 8) * 8

        def slab(k, prev):
            cur = hydro_slab(start + k)
            out = blend(cur, prev)
            for f in range(4):
                fin[start + k, f] = out[f]
            return cur

        lax.fori_loop(0, 8, slab, hydro_slab(start - 1), unroll=8)

        @pl.when(i > 0)
        def _():
            send_far(spread(i - 1), rho_message)

        @pl.when(i == 2)
        def _():
            send_far(4, vel_message)

        return carry

    lax.fori_loop(0, 8, block, 0)
    send(0, rho_message, own_rho)
    send_far(1, vel_message)
    send_far(7, vel_message)
    send(0, vel_message, own_vel)

    wait_all(rho_back.at[pl.ds(0, 63)], (rs, rr))
    own_rho.wait()
    for g in range(4):
        t = jnp.concatenate([rho_back[where_of(j, g)] for j in range(16)], axis=0).T.reshape(16, 8, 128)
        for i in range(16):
            flat[pl.ds(i * 32 + 8 * g, 8), :] = t[i]
    k = row * 128 + lax.broadcasted_iota(jnp.int32, (16, 128), 1)
    radius = R_INNER + (k.astype(F32) + 0.5) * (1.0 - R_INNER) / NR
    seen = jnp.ones((16, 128), F32)
    total = jnp.zeros((16, 128), F32)
    for j in range(NTH):
        tilt = float(np.float32(1.0 + 0.5 * np.cos(np.pi * (j + 0.5) / NTH)))
        t = jnp.exp(flat[pl.ds(j, 16, stride=32), :] * (-KAPPA / NTH))
        total = total + tilt * ((1.0 - t) * seen)
        seen = seen * t
    light[...] = (1.0 / jnp.sqrt(radius)) * total

    own_light = pltpu.make_async_copy(light, table.at[row, xy, zl], ls.at[3])
    own_light.start()

    def up(n):
        to = {"phi": (half * 4 + lax.rem(zl + n, 4)) * 8 + xy}
        return remote(light, table.at[row, xy, zl], us.at[n], ur.at[n], to)

    def over(n, end):
        to = {"phi": ((1 - half) * 4 + lax.rem(zl + n, 4)) * 8 + xy}
        return remote(light, table.at[row, 8, end], us.at[4 + n], ur.at[4 + n], to)

    ends = ((1, 0, 0), (0, 7, 3))
    for n in (2, 1, 3):
        up(n).start()
    for end, at, plane in ends:

        @pl.when((xy == at) & (zl == plane))
        def _(end=end):
            for n in range(4):
                over(n, end).start()

    for off in (3, 5, 2, 6):
        send_far(off, vel_message)
    for n in (1, 2, 3):
        up(n).wait()
    own_light.wait()
    for end, at, plane in ends:

        @pl.when((xy == at) & (zl == plane))
        def _(end=end):
            for n in range(4):
                over(n, end).wait_send()

        for pos in range(4):

            @pl.when((xy == at) & (zl == pos))
            def _(end=end, pos=pos, plane=plane):
                over((pos - plane) % 4, end).wait_recv()

    def part(q, pos, ssem, rsem, to):
        return remote(table.at[q, pos], table.at[q, pos], ssem, rsem, to)

    def outer(q, end, ssem, rsem, to):
        return remote(table.at[q, 8, end], table.at[q, 8, end], ssem, rsem, to)

    def to_chip(n, c):
        part(row, xy, ps.at[n], pr.at[n], chip(n)).start()
        for end, at, _ in ends:

            @pl.when(xy == at)
            def _(end=end):
                outer(row, end, hs.at[n], hrr.at[n], chip(n)).start()

        return c

    def give(q, pos, n):
        part(q, pos, gs.at[n], gr.at[n], sibling).start()
        for end, at, _ in ends:

            @pl.when(pos == at)
            def _(end=end):
                outer(q, end, hs.at[16 + n], hrr.at[16 + n], sibling).start()

    def source(n):
        m = lax.rem(xy * 2 + yh + 16 - n, 16)
        return m // 2, lax.rem(m, 2)

    def from_chip(n, c):
        pos, high = source(n)
        q = high * 2 + core
        part(q, pos, ps.at[n], pr.at[n], chip(n)).wait_recv()
        for end, at, _ in ends:

            @pl.when(pos == at)
            def _(end=end):
                outer(q, end, hs.at[n], hrr.at[n], chip(n)).wait_recv()

        give(q, pos, n)
        return c

    def finish(n, c):
        pos, high = source(n)
        q, other = high * 2 + core, high * 2 + 1 - core
        part(q, pos, gs.at[n], gr.at[n], sibling).wait_send()
        part(other, pos, gs.at[n], gr.at[n], sibling).wait_recv()
        for end, at, _ in ends:

            @pl.when(pos == at)
            def _(end=end):
                outer(q, end, hs.at[16 + n], hrr.at[16 + n], sibling).wait_send()
                outer(other, end, hs.at[16 + n], hrr.at[16 + n], sibling).wait_recv()

        return c

    def sent(n, c):
        part(row, xy, ps.at[n], pr.at[n], chip(n)).wait_send()
        for end, at, _ in ends:

            @pl.when(xy == at)
            def _(end=end):
                outer(row, end, hs.at[n], hrr.at[n], chip(n)).wait_send()

        return c

    lax.fori_loop(1, 16, to_chip, 0)
    give(row, xy, 0)
    lax.fori_loop(1, 16, from_chip, 0)
    lax.fori_loop(0, 16, finish, 0)
    lax.fori_loop(1, 16, sent, 0)
    wait_all(back.at[pl.ds(0, 63)], (vs, vr))
    own_vel.wait()


@functools.lru_cache(maxsize=None)
def sample_plan(rows_dev):
    yy = ((np.arange(NPIX) + 0.5) / NPIX * 2.0 - 1.0)[:, None]
    xx = ((np.arange(NPIX) + 0.5) / NPIX * 2.0 - 1.0)[None, :]
    u = (np.sqrt(xx * xx + yy * yy) - R_INNER) / (1.0 - R_INNER) * NR - 0.5
    v = (np.arctan2(yy, xx) + np.pi) / (2.0 * np.pi) * NPHI - 0.5
    blocks = NPIX // rows_dev
    plans = []
    for b in range(blocks):
        plan = []
        for c in range(NPIX // 128):
            cut = np.s_[b * rows_dev : (b + 1) * rows_dev, c * 128 : (c + 1) * 128]
            uu, vv = u[cut], v[cut]
            for q in range(NR // 128):
                hit = (uu > q * 128 - 1.01) & (uu < q * 128 + 128.01)
                if hit.any():
                    lo = int(np.floor((vv[hit].min() - 0.01) / 8))
                    hi = int(np.floor((np.floor(vv[hit].max() + 0.01) + 1) / 8))
                    plan.append((c, q, lo, hi - lo + 1))
        plans.append(plan)
    most = max(len(p) for p in plans)
    table = np.zeros((blocks, most, 4), np.int32)
    for b, plan in enumerate(plans):
        table[b, : len(plan)] = plan
    return table


def last_kernel(plan_ref, u_ref, v_ref, rho_src, vel_src, w_ref, rho_ref, vel_ref, out_ref, acc, *, most):
    phi, row = lax.axis_index("phi"), lax.axis_index("row")
    for f in range(4):
        for g in range(4):
            x = jnp.concatenate(
                [rho_src[where_of(j, g)] if f == 0 else vel_src[where_of(j, g), f - 1] for j in range(16)], axis=0
            )
            t = x.T.reshape(16, 8, 128)
            if f == 0:
                rho_ref[:, 8 * g : 8 * g + 8, :] = t
            else:
                vel_ref[f - 1, :, 8 * g : 8 * g + 8, :] = t
    spot = phi * 4 + row
    first_tile = phi // 32 * 64
    acc[...] = jnp.zeros_like(acc)
    sub = lax.broadcasted_iota(jnp.int32, (8, 128), 0)

    def task(t, carry):
        word = plan_ref[spot * most + t]
        chunk, q = word % 8, word // 8 % 4
        lo, count = word // 32 % 256 - 1, word // 8192
        cols = pl.ds(pl.multiple_of(chunk * 128, 128), 128)
        u, v = u_ref[:, cols], v_ref[:, cols]
        floor = jnp.floor(u)
        part = u - floor
        k = floor.astype(jnp.int32) - q * 128 + jnp.where(sub >= 4, 1, 0)
        weight = jnp.where(sub >= 4, part, 1.0 - part)
        weight = jnp.where((k >= 0) & (k < 128), weight, 0.0)
        k = jnp.clip(k, 0, 127)

        def tile(near, total):
            shifted = v - ((near + first_tile) * 8).astype(F32)
            slab = jnp.where(near < 0, 32, jnp.where(near > 63, 33, near // 2 % 8 * 4 + near // 16))
            start = pl.multiple_of(slab * 16 + (near + 2) % 2 * 8, 8)
            for s in range(8):
                line = jnp.broadcast_to(w_ref[q, pl.ds(start + s, 1), :], (8, 128))
                got = jnp.take_along_axis(line, k, axis=1, mode="promise_in_bounds")
                total = total + jnp.maximum(1.0 - jnp.abs(shifted - float(s)), 0.0) * got
            return total

        def pair(i, totals):
            near = lo - first_tile + 4 * i
            return tuple(tile(near + i, t) for i, t in enumerate(totals))

        nothing = jnp.zeros((8, 128), F32)
        a, b, c, d = lax.fori_loop(0, (count + 3) // 4, pair, (nothing,) * 4)
        total = (a + b) + (c + d)
        acc[:, cols] = acc[:, cols] + weight * total
        return carry

    lax.fori_loop(0, most, task, 0)
    out_ref[...] = acc[0:4, :] + acc[4:8, :]


def body(density, velocity, shifts, fractions):
    sds = lambda *s: jax.ShapeDtypeStruct(s, F32)
    dma = lambda *s: pltpu.SemaphoreType.DMA(s)
    vmem = lambda *s: pltpu.VMEM(s, F32)
    one = pltpu.SemaphoreType.DMA
    back, table, rho_back, upos, vpos = pl.pallas_call(
        main_kernel, name="main", out_shape=(sds(64, 3, 8, 128), sds(4, 9, 4, 16, 128), sds(64, 8, 128), sds(8, 1024), sds(8, 1024)),
        in_specs=[SM, SM, ANY, ANY], out_specs=(ANY, ANY, VM, VM, VM),
        scratch_shapes=[
            vmem(16, 32, 128), vmem(3, 16, 32, 128), vmem(4, 4, 144, 128), vmem(2, 16, 128), vmem(2, 4, 32, 128), vmem(2, 16, 128), vmem(2, 128, 128),
            vmem(64, 4, 8, 128), vmem(64, 4, 8, 128), vmem(64, 4, 8, 128),
            vmem(2, 8, 4, 8, 128), vmem(2, 64, 4, 128), vmem(2, 8, 4, 8, 128), vmem(2, 64, 4, 128),
            vmem(64, 4, 8, 128), vmem(512, 128), vmem(16, 128),
            pltpu.SemaphoreType.REGULAR((3,)), dma(6), dma(6), one, one, dma(4), dma(4), one, one, one, one, dma(6), dma(8), dma(8),
            dma(32), dma(32), dma(16), dma(16), dma(16), dma(16),
        ],
        compiler_params=pltpu.CompilerParams(collective_id=0, has_side_effects=True),
    )(shifts, fractions, density, velocity)
    plan = sample_plan(4)
    most = plan.shape[1]
    words = plan[..., 0] + 8 * plan[..., 1] + 32 * (plan[..., 2] + 1) + 8192 * plan[..., 3]
    return pl.pallas_call(
        functools.partial(last_kernel, most=most), name="last",
        out_shape=(sds(16, 32, 128), sds(3, 16, 32, 128), sds(4, 1024)),
        in_specs=[SM, VM, VM, VM, VM, VM], out_specs=(VM, VM, VM),
        scratch_shapes=[pltpu.VMEM((8, 1024), F32)],
    )(jnp.asarray(words.reshape(-1)), upos, vpos, rho_back, back, table.reshape(4, 576, 128))


def solution(mesh):
    in_specs = (P("phi", None, "row"), P(None, "phi", None, "row"), P("row"), P("row"))
    out_specs = (P("phi", None, "row"), P(None, "phi", None, "row"), P(("phi", "row"), None))
    return jax.shard_map(body, mesh=mesh, in_specs=in_specs, out_specs=out_specs, check_vma=False)
```
